256 devices in a mesh: section: 4 (over x), shard: 64 (over z, y, core).
Axes of the slice: x: 4, y: 4, z: 8, core: 2. Of those that a mesh axis runs over, the one named last changes fastest.
Arguments:
- voltages: bfloat16 [4, 2, 1024, 32768], P('section', None, 'shard'), may hold values from -30 to 30, as said below
- feed_gains: bfloat16 [2, 1024, 1024], P(None, 'shard'), may hold values from -6 to 6
- grid_index: int32 [1024], replicated, may hold values from 0 to 1023, each once
- decay_rates: float32 [1024], P('shard'), may hold values from 0.3 to 0.95
- delays: int32 [1024, 512], replicated, may hold values from 0 to 4095
Outputs:
- dedispersed: bfloat16 [4, 7, 512, 2, 1024], P('section', None, None, None, 'shard')
The draws below stay inside these ranges and needn't reach their ends.
Inputs may be any that keep to these rules, and one draw needn't show every extreme that they name: Real sample voltages.
All inputs are finite; a program needn't handle non-finite values.
Results may differ from the reference program's by a relative error of at most 0.009.
Values may be sent and summed in bfloat16 or wider, within the bound.
A program may use at most 192 MiB of HBM per device.

```python
import math
import jax
import jax.numpy as jnp
from jax import lax

POL = 2
GRID_X = 4
GRID_Y = 256
NSAMP = 2048
TDFT = 16
TRIALS = 512
FEEDS = 1024
CHANS = 1024
MODF = 7
BLOCKS = 4


def draw_voltages(key, part):
    key_noise = jax.random.fold_in(key, 11)
    key_level = jax.random.fold_in(key, 12)
    key_rise = jax.random.fold_in(key, 13)
    shape = (BLOCKS, POL, FEEDS, TDFT * NSAMP)
    jitter = jax.random.uniform(key_rise, (BLOCKS,), jnp.float32, 0.0, 1.0)
    block_rise = 3.0 ** ((jnp.arange(BLOCKS, dtype=jnp.float32) + jitter) / BLOCKS)
    block_rise = block_rise[:, None, None, None]
    feed_level = jnp.exp(jax.random.uniform(key_level, (1, POL, FEEDS, 1), jnp.float32, math.log(0.5), math.log(2.0)))
    fluctuation = jnp.clip(jax.random.normal(key_noise, shape, jnp.float32), -5.0, 5.0)
    return (fluctuation * block_rise * feed_level).astype(jnp.bfloat16)


def set_ends(entries, stream_key, least, largest):
    longest = entries.shape.index(max(entries.shape))
    spots = []
    for shift in (0, 1):
        where = [jax.random.randint(jax.random.fold_in(stream_key, axis), (), 0, length) for axis, length in enumerate(entries.shape)]
        where[longest] = (where[longest] + shift) % entries.shape[longest]
        spots.append(tuple(where))
    return entries.at[spots[0]].set(least).at[spots[1]].set(largest)


def block_levels(own_key, extent, pieces, low, top_value):
    def one(axis_at, parts):
        draws = jax.random.uniform(jax.random.fold_in(jax.random.fold_in(own_key, 6), axis_at), (parts,), jnp.float32, low / len(pieces), top_value / len(pieces))
        return jnp.repeat(jnp.exp(draws), extent[axis_at] // parts).reshape((-1,) + (1,) * (len(extent) - axis_at - 1))

    factor_of = one(*pieces[0])
    for cut in pieces[1:]:
        factor_of = factor_of * one(*cut)
    return factor_of


def centred(rng, extent, spread, limit, cuts=(), held_as=jnp.bfloat16):
    entries = jax.random.normal(rng, extent, jnp.float32) * spread
    if len(cuts) > 0:
        entries = block_levels(rng, extent, cuts, -0.22, 0.18) * entries
    return jnp.clip(entries, min=-limit, max=limit).astype(held_as)


def setup_inputs(seed: int = 0) -> dict:
    keys = jax.random.split(jax.random.key(seed), 6)
    voltages = draw_voltages(jax.random.fold_in(keys[5], 71), 0)
    feed_gains = centred(keys[1], (2, CHANS, FEEDS), 1.0, 6.0, ((1, 64),))
    grid_index = jax.random.permutation(keys[2], FEEDS).astype(jnp.int32)
    decay_rates = jnp.clip(0.3 + 0.65 * jax.random.uniform(keys[3], (CHANS,), jnp.float32) ** block_levels(keys[3], (CHANS,), ((0, 64),), -0.2, 0.2), 0.3, 0.95)
    delays = set_ends(jax.random.randint(keys[4], (CHANS, TRIALS), 0, 4096), jax.random.fold_in(keys[4], 1), 0, 4095).astype(jnp.int32)
    return {"voltages": voltages, "feed_gains": feed_gains, "grid_index": grid_index, "decay_rates": decay_rates, "delays": delays}


def spectral_table():
    row_index = jnp.arange(CHANS, dtype=jnp.int32)[:, None]
    col_index = jnp.arange(NSAMP, dtype=jnp.int32)[None, :]
    angles = 2.0 * math.pi / NSAMP * (row_index * col_index % NSAMP).astype(jnp.float32)
    return jnp.concatenate([jnp.cos(angles), -jnp.sin(angles)], 0).astype(jnp.bfloat16)

def twiddle_table(length):
    row_index = jnp.arange(length, dtype=jnp.int32)[:, None]
    col_index = jnp.arange(length, dtype=jnp.int32)[None, :]
    angles = 2.0 * math.pi / length * (row_index * col_index % length).astype(jnp.float32)
    cosine = jnp.cos(angles)
    sine = jnp.sin(angles)
    return jnp.stack([jnp.stack([cosine, -sine], 1), jnp.stack([sine, cosine], 1)], 0)

def frame_table():
    frames = jnp.arange(TDFT, dtype=jnp.int32)[:, None]
    freqs = jnp.arange(1, MODF + 1, dtype=jnp.int32)[None, :]
    angles = 2.0 * math.pi / TDFT * (frames * freqs % TDFT).astype(jnp.float32)
    return jnp.concatenate([jnp.cos(angles), -jnp.sin(angles)], 1) / math.sqrt(TDFT)

def form_beams(transposed_block, feed_gains, cell_feed):
    chan_count = transposed_block.shape[1]
    pol_count = transposed_block.shape[2]
    values = transposed_block.reshape(2, chan_count, pol_count, FEEDS, TDFT).astype(jnp.float32)
    gain_values = feed_gains.astype(jnp.float32)[:, :, None, :, None]
    real_part = gain_values[0] * values[0] - gain_values[1] * values[1]
    imag_part = gain_values[0] * values[1] + gain_values[1] * values[0]
    calibrated = jnp.stack([real_part, imag_part]).astype(jnp.bfloat16)
    gridded = jnp.take(calibrated, cell_feed, axis=3).reshape(2, chan_count, pol_count, GRID_X, GRID_Y, TDFT)
    rows = twiddle_table(GRID_Y).astype(jnp.bfloat16)
    row_beams = jnp.einsum('acpxyn,aybw->bcpxwn', gridded.astype(jnp.float32), rows.astype(jnp.float32))
    beam_voltage = jnp.einsum('bcpxwn,bxeu->ecpnuw', row_beams, twiddle_table(GRID_X), precision=lax.Precision.HIGHEST)
    powers = lax.optimization_barrier(jnp.sum(beam_voltage * beam_voltage, axis=0))
    return jnp.moveaxis(powers, 1, 0).reshape(pol_count, chan_count, TDFT, FEEDS)

def dedisperse(modulated, delays):

    def per_frequency(position_index):
        frequency = position_index + 1
        angles = 2.0 * math.pi / TDFT * (frequency * delays % TDFT).astype(jnp.float32)
        phases = jnp.concatenate([jnp.cos(angles), jnp.sin(angles)], 0).astype(jnp.bfloat16)
        mod_real = modulated[:, :, position_index]
        modulated_imaginary = modulated[:, :, MODF + position_index]
        stacked = jnp.concatenate([jnp.concatenate([mod_real, modulated_imaginary], 1), jnp.concatenate([modulated_imaginary, -mod_real], 1)], 0)
        result = lax.dot_general(phases, stacked, (((0,), (0,)), ((), ())), preferred_element_type=jnp.float32) / math.sqrt(CHANS)
        return result.reshape(TRIALS, 2, modulated.shape[1]).astype(jnp.bfloat16)
    return lax.map(per_frequency, jnp.arange(MODF, dtype=jnp.int32))

def reference(voltages, feed_gains, grid_index, decay_rates, delays):
    cell_feed = jnp.zeros((FEEDS,), jnp.int32).at[grid_index].set(jnp.arange(FEEDS, dtype=jnp.int32))
    spectral_rows = spectral_table()

    def block_energy(block_volts):
        samples = block_volts.reshape(POL * FEEDS * TDFT, NSAMP)
        spectra = lax.dot_general(spectral_rows, samples, (((1,), (1,)), ((), ())), preferred_element_type=jnp.float32)
        spectra = (spectra * (1.0 / math.sqrt(NSAMP))).astype(jnp.bfloat16).reshape(2, CHANS, POL, FEEDS * TDFT)
        return lax.optimization_barrier(jnp.sum(form_beams(spectra, feed_gains, cell_feed), axis=0))
    beam_power = lax.map(block_energy, voltages)
    levels = lax.optimization_barrier(jnp.mean(beam_power, axis=(2, 3))) + 1e-06
    ratio_dividend = jnp.zeros((CHANS,), jnp.float32)
    ratio_divisor = jnp.zeros((CHANS,), jnp.float32)
    baseline_levels = []
    for block in range(BLOCKS):
        ratio_dividend = decay_rates * ratio_dividend + levels[block]
        ratio_divisor = decay_rates * ratio_divisor + 1.0
        baseline_levels.append(ratio_dividend / ratio_divisor)
    baseline_level = jnp.stack(baseline_levels)

    def finish(inputs):
        block_power_values, block_base = inputs
        normalized = block_power_values / block_base[:, None, None] - 1.0
        modulated = jnp.einsum('cnb,nq->cbq', normalized, frame_table(), precision=lax.Precision.HIGHEST).astype(jnp.bfloat16)
        return dedisperse(modulated, delays)
    return lax.map(finish, (beam_power, baseline_level))
```

```python
import math

import jax
import jax.numpy as jnp
import numpy as np
from jax import lax
from jax.experimental import pallas as pl
from jax.experimental.pallas import tpu as pltpu
from jax.sharding import PartitionSpec as P

POL = 2
GRID_X = 4
GRID_Y = 256
NSAMP = 2048
TDFT = 16
TRIALS = 512
FEEDS = 1024
CHANS = 1024
MODF = 7
BLOCKS = 4
SHARDS = 64
LOCAL = 16
VMEM_LIMIT = 56 * 1024 * 1024


def spectral_constant():
    dest, part, chan = np.meshgrid(np.arange(SHARDS), np.arange(2), np.arange(LOCAL), indexing="ij")
    chans = (dest * LOCAL + chan).reshape(-1).astype(np.int64)
    part = part.reshape(-1)
    cols = np.arange(NSAMP, dtype=np.int64)[None, :]
    angles = np.float32(2.0 * math.pi / NSAMP) * (chans[:, None] * cols % NSAMP).astype(np.float32)
    table = np.where(part[:, None] == 0, np.cos(angles), -np.sin(angles)).astype(np.float32)
    return jnp.asarray(table).astype(jnp.bfloat16)


def row_constant():
    rows = np.arange(GRID_Y)[:, None]
    cols = np.arange(GRID_Y)[None, :]
    angles = np.float32(2.0 * math.pi / GRID_Y) * (rows * cols % GRID_Y).astype(np.float32)
    table = np.concatenate([np.cos(angles), np.sin(angles)], 1).astype(np.float32)
    return jnp.asarray(table).astype(jnp.bfloat16)


def frame_matrix():
    frames = np.arange(TDFT)[:, None]
    freqs = np.arange(1, MODF + 1)[None, :]
    angles = 2.0 * math.pi / TDFT * (frames * freqs % TDFT)
    return np.concatenate([np.cos(angles), -np.sin(angles)], 1) / math.sqrt(TDFT)


def channelize_body(table_ref, volts_ref, out_ref, rows_ref):
    @pl.when(pl.program_id(0) == 0)
    def _():
        for pol in range(POL):
            for frame in range(TDFT):
                start = (pol * TDFT + frame) * LOCAL
                rows_ref[start : start + LOCAL, :] = volts_ref[
                    pol, :, frame * NSAMP : (frame + 1) * NSAMP
                ]

    spectra = lax.dot_general(
        table_ref[...], rows_ref[...], (((1,), (1,)), ((), ())), preferred_element_type=jnp.float32
    )
    out_ref[...] = (spectra * (1.0 / math.sqrt(NSAMP))).astype(jnp.bfloat16)


def channelize(volts):
    block = 256
    lanes = POL * TDFT * LOCAL
    return pl.pallas_call(
        channelize_body,
        out_shape=jax.ShapeDtypeStruct((2 * CHANS, lanes), jnp.bfloat16),
        grid=(2 * CHANS // block,),
        in_specs=[
            pl.BlockSpec((block, NSAMP), lambda i: (i, 0)),
            pl.BlockSpec((POL, LOCAL, TDFT * NSAMP), lambda i: (0, 0, 0)),
        ],
        out_specs=pl.BlockSpec((block, lanes), lambda i: (i, 0)),
        scratch_shapes=[pltpu.VMEM((lanes, NSAMP), jnp.bfloat16)],
        compiler_params=pltpu.CompilerParams(vmem_limit_bytes=VMEM_LIMIT),
        name="channelize",
    )(spectral_constant(), volts)


def cosine_of(step):
    fold = jnp.abs(8 - step)
    out = jnp.full(step.shape, -math.cos(0.0), jnp.float32)
    for entry in range(1, 9):
        out = jnp.where(fold == entry, np.float32(-math.cos(2.0 * math.pi * entry / TDFT)), out)
    return out


def phase_body(delay_ref, out_ref):
    step = delay_ref[...] & (TDFT - 1)
    cos_one = cosine_of(step)
    sin_one = cosine_of((step + 12) & (TDFT - 1))
    twice = 2.0 * cos_one
    cos_now, sin_now = cos_one, sin_one
    cos_last, sin_last = jnp.ones_like(cos_one), jnp.zeros_like(cos_one)
    for f in range(MODF):
        out_ref[f, 0] = cos_now.astype(jnp.bfloat16)
        out_ref[f, 1] = sin_now.astype(jnp.bfloat16)
        cos_now, cos_last = twice * cos_now - cos_last, cos_now
        sin_now, sin_last = twice * sin_now - sin_last, sin_now


def phase_tables(delays):
    block = 64
    return pl.pallas_call(
        phase_body,
        out_shape=jax.ShapeDtypeStruct((MODF, 2, CHANS, TRIALS), jnp.bfloat16),
        grid=(CHANS // block,),
        in_specs=[pl.BlockSpec((block, TRIALS), lambda i: (i, 0))],
        out_specs=pl.BlockSpec((MODF, 2, block, TRIALS), lambda i: (0, 0, i, 0)),
        compiler_params=pltpu.CompilerParams(vmem_limit_bytes=VMEM_LIMIT),
        name="phases",
    )(delays)


def beam_table_body(cell_ref, rows_ref, out_ref):
    cell = cell_ref[...]
    x = cell // GRID_Y
    y = cell % GRID_Y
    hot = (lax.broadcasted_iota(jnp.int32, (cell.shape[0], GRID_Y), 1) == y).astype(jnp.float32)
    both = jnp.dot(
        hot.astype(jnp.bfloat16), rows_ref[...], preferred_element_type=jnp.float32
    )
    cos, sin = both[:, :GRID_Y], both[:, GRID_Y:]
    for u in range(GRID_X):
        turn = (u * x) & 3
        real = jnp.where(turn == 0, cos, jnp.where(turn == 1, -sin, jnp.where(turn == 2, -cos, sin)))
        imag = jnp.where(turn == 0, -sin, jnp.where(turn == 1, -cos, jnp.where(turn == 2, sin, cos)))
        out_ref[0, :, u * GRID_Y : (u + 1) * GRID_Y] = real.astype(jnp.bfloat16)
        out_ref[1, :, u * GRID_Y : (u + 1) * GRID_Y] = imag.astype(jnp.bfloat16)


def beam_table(grid_index):
    block = 256
    return pl.pallas_call(
        beam_table_body,
        out_shape=jax.ShapeDtypeStruct((2, FEEDS, FEEDS), jnp.bfloat16),
        grid=(FEEDS // block,),
        in_specs=[
            pl.BlockSpec((block, 1), lambda i: (i, 0)),
            pl.BlockSpec((GRID_Y, 2 * GRID_Y), lambda i: (0, 0)),
        ],
        out_specs=pl.BlockSpec((2, block, FEEDS), lambda i: (0, i, 0)),
        compiler_params=pltpu.CompilerParams(vmem_limit_bytes=VMEM_LIMIT),
        name="beam_table",
    )(grid_index.reshape(FEEDS, 1), row_constant())


def exchange(parts):
    parts = list(parts)
    lane = lax.broadcasted_iota(jnp.int32, parts[0].shape, 1)
    for bit in (4, 2, 1):
        upper = (lane & (bit * LOCAL)) != 0
        for i in range(8):
            if i & bit:
                continue
            low, high = parts[i], parts[i + bit]
            parts[i] = jnp.where(upper, pltpu.roll(high, bit * LOCAL, 1), low)
            parts[i + bit] = jnp.where(upper, high, pltpu.roll(low, 128 - bit * LOCAL, 1))
    return parts


def calibrate_body(data_ref, gain_ref, out_ref, level_ref, sum_ref):
    octet = pl.program_id(0)
    gain_real = gain_ref[0].astype(jnp.float32)
    gain_imag = gain_ref[1].astype(jnp.float32)

    def one(tile, total):
        lanes = pl.ds(pl.multiple_of(tile * 128, 128), 128)
        parts = [data_ref[s, :, lanes].astype(jnp.float32) for s in range(8)]
        parts = exchange(parts)
        for n, part in enumerate(parts):
            real, imag = part[:LOCAL], part[LOCAL:]
            cal_real = (gain_real * real - gain_imag * imag).astype(jnp.bfloat16)
            cal_imag = (gain_real * imag + gain_imag * real).astype(jnp.bfloat16)
            rows = pl.ds(pl.multiple_of(tile * 128 + n * LOCAL, LOCAL), LOCAL)
            out_ref[0, rows, :] = cal_real
            out_ref[1, rows, :] = cal_imag
            wide_real, wide_imag = cal_real.astype(jnp.float32), cal_imag.astype(jnp.float32)
            total = total + (wide_real * wide_real + wide_imag * wide_imag)
        return total

    total = lax.fori_loop(0, 4, one, jnp.zeros((LOCAL, 128), jnp.float32))

    @pl.when(octet == 0)
    def _():
        sum_ref[...] = jnp.zeros_like(sum_ref)

    sum_ref[...] += total

    @pl.when(octet == 7)
    def _():
        level = jnp.sum(sum_ref[...], axis=1, keepdims=True) * (1.0 / TDFT) + 1e-06
        level_ref[...] = jnp.broadcast_to(level, level_ref.shape)


def calibrate(turned, feed_gains):
    rows = POL * TDFT * LOCAL
    return pl.pallas_call(
        calibrate_body,
        out_shape=(
            jax.ShapeDtypeStruct((2, rows, FEEDS), jnp.bfloat16),
            jax.ShapeDtypeStruct((LOCAL, 128), jnp.float32),
        ),
        grid=(8,),
        in_specs=[
            pl.BlockSpec((8, 2 * LOCAL, rows), lambda i: (i, 0, 0)),
            pl.BlockSpec((2, LOCAL, 128), lambda i: (0, 0, i)),
        ],
        out_specs=(
            pl.BlockSpec((2, rows, 128), lambda i: (0, 0, i)),
            pl.BlockSpec((LOCAL, 128), lambda i: (0, 0)),
        ),
        scratch_shapes=[pltpu.VMEM((LOCAL, 128), jnp.float32)],
        compiler_params=pltpu.CompilerParams(vmem_limit_bytes=VMEM_LIMIT),
        name="calibrate",
    )(turned, feed_gains)


def frame_transform(power):
    half = TDFT // 2
    table = frame_matrix()
    plus = [power[n] + power[n + half] for n in range(half)]
    minus = [power[n] - power[n + half] for n in range(half)]
    out = []
    for q in range(2 * MODF):
        source = minus if (q % MODF + 1) % 2 else plus
        total = None
        for n in range(half):
            factor = float(table[n, q])
            if abs(factor) < 1e-12:
                continue
            term = source[n] * np.float32(factor)
            total = term if total is None else total + term
        out.append(total)
    return out


def beam_body(cal_ref, table_ref, scale_ref, out_ref, power_ref):
    half = POL * TDFT * LOCAL // 2
    cal_real, cal_imag = cal_ref[0], cal_ref[1]
    real_table, imag_table = table_ref[0], table_ref[1]

    def mul(a, b):
        return jnp.dot(a, b, preferred_element_type=jnp.float32)

    real = mul(cal_real, real_table) - mul(cal_imag, imag_table)
    imag = mul(cal_real, imag_table) + mul(cal_imag, real_table)
    power = real * real + imag * imag
    power_ref[...] = power[:half] + power[half:]
    offset = frame_matrix().sum(0)
    scale = scale_ref[...]
    for tile in range(power_ref.shape[1] // 128):
        lanes = slice(tile * 128, (tile + 1) * 128)
        frames = [power_ref[n * LOCAL : (n + 1) * LOCAL, lanes] for n in range(TDFT)]
        freqs = frame_transform(frames)
        freqs = [v * scale - np.float32(offset[q]) for q, v in enumerate(freqs)]
        freqs = freqs + [jnp.zeros_like(freqs[0])] * 2
        for group in range(2):
            for j, part in enumerate(exchange(freqs[group * 8 : group * 8 + 8])):
                out_ref[tile * 8 + j, :, group * 128 : (group + 1) * 128] = part.astype(jnp.bfloat16)


def form_beams(calibrated, table, scale):
    block = 256
    rows = POL * TDFT * LOCAL
    return pl.pallas_call(
        beam_body,
        out_shape=jax.ShapeDtypeStruct((SHARDS, LOCAL, 256), jnp.bfloat16),
        grid=(FEEDS // block,),
        in_specs=[
            pl.BlockSpec((2, rows, FEEDS), lambda i: (0, 0, 0)),
            pl.BlockSpec((2, FEEDS, block), lambda i: (0, 0, i)),
            pl.BlockSpec((LOCAL, 128), lambda i: (0, 0)),
        ],
        out_specs=pl.BlockSpec((block // LOCAL, LOCAL, 256), lambda i: (i, 0, 0)),
        scratch_shapes=[pltpu.VMEM((rows // 2, block), jnp.float32)],
        compiler_params=pltpu.CompilerParams(vmem_limit_bytes=VMEM_LIMIT),
        name="beams",
    )(calibrated, table, scale)


def dedisperse_body(data_ref, phase_ref, out_ref, turned_ref):
    f = pl.program_id(0)

    @pl.when(f == 0)
    def _():
        turned_ref[...] = data_ref[...].astype(jnp.float32).T.astype(jnp.bfloat16)

    real = turned_ref[pl.ds(pl.multiple_of(f * LOCAL, LOCAL), LOCAL), :]
    imag = turned_ref[pl.ds(pl.multiple_of((f + MODF) * LOCAL, LOCAL), LOCAL), :]
    with_cos = jnp.concatenate([real, imag], 0)
    with_sin = jnp.concatenate([imag, -real], 0)
    total = jnp.dot(with_cos, phase_ref[0, 0], preferred_element_type=jnp.float32)
    total = total + jnp.dot(with_sin, phase_ref[0, 1], preferred_element_type=jnp.float32)
    out_ref[0] = (total * (1.0 / math.sqrt(CHANS))).astype(jnp.bfloat16)


def dedisperse(data, phases):
    return pl.pallas_call(
        dedisperse_body,
        out_shape=jax.ShapeDtypeStruct((MODF, 2 * LOCAL, TRIALS), jnp.bfloat16),
        grid=(MODF,),
        in_specs=[
            pl.BlockSpec((CHANS, 256), lambda i: (0, 0)),
            pl.BlockSpec((1, 2, CHANS, TRIALS), lambda i: (i, 0, 0, 0)),
        ],
        out_specs=pl.BlockSpec((1, 2 * LOCAL, TRIALS), lambda i: (i, 0, 0)),
        scratch_shapes=[pltpu.VMEM((256, CHANS), jnp.bfloat16)],
        compiler_params=pltpu.CompilerParams(vmem_limit_bytes=VMEM_LIMIT),
        name="dedisperse",
    )(data, phases)


def shards(voltages, feed_gains, grid_index, decay_rates, delays):
    spectra = channelize(voltages[0]).reshape(SHARDS, 2 * LOCAL, POL * TDFT * LOCAL)
    turned = lax.all_to_all(spectra, "shard", split_axis=0, concat_axis=0, tiled=True)
    phases = phase_tables(delays)
    table = beam_table(grid_index)
    calibrated, levels = calibrate(turned, feed_gains)
    gathered = lax.all_gather(levels[:, 0], "section")
    place = lax.axis_index("section")
    dividend = jnp.zeros_like(decay_rates)
    divisor = jnp.zeros_like(decay_rates)
    for block in range(BLOCKS):
        use = block <= place
        dividend = jnp.where(use, decay_rates * dividend + gathered[block], dividend)
        divisor = jnp.where(use, decay_rates * divisor + 1.0, divisor)
    scale = jnp.broadcast_to((divisor / dividend)[:, None], (LOCAL, 128))
    modulated = form_beams(calibrated, table, scale)
    moved = lax.all_to_all(modulated, "shard", split_axis=0, concat_axis=0, tiled=True)
    out = dedisperse(moved.reshape(CHANS, 256), phases)
    return out.reshape(MODF, 2, LOCAL, TRIALS).transpose(0, 3, 1, 2)[None]


def solution(mesh):
    in_specs = (P("section", None, "shard", None), P(None, "shard", None), P(), P("shard"), P())
    out_specs = P("section", None, None, None, "shard")
    return jax.shard_map(shards, mesh=mesh, in_specs=in_specs, out_specs=out_specs, check_vma=False)
```

```python
import math

import jax
import jax.numpy as jnp
import numpy as np
from jax import lax
from jax.experimental import pallas as pl
from jax.experimental.pallas import tpu as pltpu
from jax.sharding import PartitionSpec as P

POL = 2
GRID_X = 4
GRID_Y = 256
NSAMP = 2048
TDFT = 16
TRIALS = 512
FEEDS = 1024
CHANS = 1024
MODF = 7
BLOCKS = 4
SHARDS = 64
LOCAL = 16
HALF = LOCAL // 2
ROWS = POL * TDFT * LOCAL
FOLD = NSAMP // 2
VMEM_LIMIT = 62 * 1024 * 1024
MESH = pl.DeviceIdType.MESH


def spectral_constant():
    shape = (2, SHARDS, 2, HALF)
    parity, dest, part, chan = np.meshgrid(*[np.arange(n) for n in shape], indexing="ij")
    chans = (dest * LOCAL + 2 * chan + parity)[..., None].astype(np.int64)
    cols = np.arange(FOLD, dtype=np.int64)
    angles = np.float32(2.0 * math.pi / NSAMP) * (chans * cols % NSAMP).astype(np.float32)
    table = np.where(part[..., None] == 0, np.cos(angles), -np.sin(angles)).astype(np.float32)
    return jnp.asarray(table.reshape(2, CHANS, FOLD)).astype(jnp.bfloat16)


def row_constant():
    rows = np.arange(GRID_Y)[:, None]
    cols = np.arange(GRID_Y)[None, :]
    angles = np.float32(2.0 * math.pi / GRID_Y) * (rows * cols % GRID_Y).astype(np.float32)
    table = np.concatenate([np.cos(angles), np.sin(angles)], 1).astype(np.float32)
    return jnp.asarray(table).astype(jnp.bfloat16)


def frame_matrix():
    frames = np.arange(TDFT)[:, None]
    freqs = np.arange(1, MODF + 1)[None, :]
    angles = 2.0 * math.pi / TDFT * (frames * freqs % TDFT)
    return np.concatenate([np.cos(angles), -np.sin(angles)], 1) / math.sqrt(TDFT)


def cosine_of(step):
    fold = jnp.abs(8 - step)
    out = jnp.full(step.shape, -math.cos(0.0), jnp.float32)
    for entry in range(1, 9):
        out = jnp.where(fold == entry, np.float32(-math.cos(2.0 * math.pi * entry / TDFT)), out)
    return out


def exchange(parts):
    parts = list(parts)
    lane = lax.broadcasted_iota(jnp.int32, parts[0].shape, 1)
    for bit in (4, 2, 1):
        upper = (lane & (bit * LOCAL)) != 0
        for i in range(8):
            if i & bit:
                continue
            low, high = parts[i], parts[i + bit]
            parts[i] = jnp.where(upper, pltpu.roll(high, bit * LOCAL, 1), low)
            parts[i + bit] = jnp.where(upper, high, pltpu.roll(low, 128 - bit * LOCAL, 1))
    return parts


def frame_transform(power):
    half = TDFT // 2
    table = frame_matrix()
    plus = [power[n] + power[n + half] for n in range(half)]
    minus = [power[n] - power[n + half] for n in range(half)]
    out = []
    for q in range(2 * MODF):
        source = minus if (q % MODF + 1) % 2 else plus
        total = None
        for n in range(half):
            factor = float(table[n, q])
            if abs(factor) < 1e-12:
                continue
            term = source[n] * np.float32(factor)
            total = term if total is None else total + term
        out.append(total)
    return out


def dot(a, b):
    return jnp.dot(a, b, preferred_element_type=jnp.float32)


def column(row):
    shape = (128, 128)
    same = lax.broadcasted_iota(jnp.int32, shape, 0) == lax.broadcasted_iota(jnp.int32, shape, 1)
    return jnp.sum(jnp.where(same, jnp.broadcast_to(row, shape), 0.0), axis=1, keepdims=True)


def body(
    volts_hbm, table_hbm, gain_hbm, delay_hbm, cell_ref, decay_ref, row_ref, out_ref,
    volts, table, gain_in, delay, folded, send, recv, gain, cal, beam_tab, phase, power,
    send_two, recv_two, turned, total_ref, level_send, level_recv,
    load_sem, own_sem, send_sem, recv_sem, send_two_sem, recv_two_sem, level_send_sem, level_recv_sem,
):
    me = lax.axis_index("shard")
    place = lax.axis_index("section")
    my_z, low = me // 8, me % 8

    loads = [
        pltpu.make_async_copy(volts_hbm.at[0], volts.at[0], load_sem.at[0]),
        pltpu.make_async_copy(table_hbm.at[0], table.at[0], load_sem.at[1]),
        pltpu.make_async_copy(volts_hbm.at[1], volts.at[1], load_sem.at[2]),
        pltpu.make_async_copy(table_hbm.at[1], table.at[1], load_sem.at[3]),
        pltpu.make_async_copy(gain_hbm, gain_in, load_sem.at[4]),
    ] + [
        pltpu.make_async_copy(
            delay_hbm.at[:, pl.ds(tile * 128, 128)], delay.at[tile], load_sem.at[5 + tile]
        )
        for tile in range(4)
    ]
    for load in loads:
        load.start()

    barrier = pltpu.get_barrier_semaphore()

    def greet(i, carry):
        pl.semaphore_signal(barrier, inc=1, device_id={"shard": (me + i) % SHARDS}, device_id_type=MESH)
        return carry

    lax.fori_loop(1, SHARDS, greet, 0)
    for i in range(1, BLOCKS):
        pl.semaphore_signal(
            barrier, inc=1, device_id={"section": (place + i) % BLOCKS}, device_id_type=MESH
        )

    for pol in range(POL):
        loads[2 * pol].wait()

        def fold(frame, carry):
            first = pl.ds(pl.multiple_of(frame * NSAMP, NSAMP), FOLD)
            second = pl.ds(pl.multiple_of(frame * NSAMP + FOLD, FOLD), FOLD)
            a = volts[pol, :, first].astype(jnp.float32)
            b = volts[pol, :, second].astype(jnp.float32)
            rows = pl.ds(pl.multiple_of((pol * TDFT + frame) * LOCAL, LOCAL), LOCAL)
            folded[0, rows, :] = (a + b).astype(jnp.bfloat16)
            folded[1, rows, :] = (a - b).astype(jnp.bfloat16)
            return carry

        lax.fori_loop(0, TDFT, fold, 0)

    def plane_of(i):
        step, odd = i // 2, i % 2
        return (my_z + 4 + step - odd * (2 * step + 1) + 8) % 8

    def send_one(half, dest):
        pltpu.make_async_remote_copy(
            send.at[half, dest], recv.at[half, me], send_sem.at[half], recv_sem.at[half, my_z],
            device_id={"shard": dest}, device_id_type=MESH,
        ).start()

    def send_plane(half, i):
        z = plane_of(i)

        def one(r, carry):
            send_one(half, z * 8 + (low + r) % 8)
            return carry

        lax.fori_loop(0, 8, one, 0)

    own = [
        pltpu.make_async_copy(send.at[half, me], recv.at[half, me], own_sem.at[half])
        for half in range(2)
    ]

    for half in range(2):
        loads[1 + 2 * half].wait()

        def channelize(i, carry):
            z = plane_of(i)
            rows = pl.ds(pl.multiple_of(z * 128, 128), 128)
            spectra = lax.dot_general(
                table[half, rows, :], folded[half], (((1,), (1,)), ((), ())),
                preferred_element_type=jnp.float32,
            )
            spectra = (spectra * (1.0 / math.sqrt(NSAMP))).astype(jnp.bfloat16)
            send[half, pl.ds(pl.multiple_of(z * 8, 8), 8)] = spectra.reshape(8, LOCAL, ROWS)

            @pl.when(i > 0)
            def _():
                if half == 0:

                    @pl.when(i == 1)
                    def _():
                        pl.semaphore_wait(barrier, SHARDS - 1 + BLOCKS - 1)

                send_plane(half, i - 1)

            return carry

        lax.fori_loop(0, 8, channelize, 0)

        def last(r, carry):
            send_one(half, my_z * 8 + (low + r) % 8)
            return carry

        lax.fori_loop(1, 8, last, 0)
        own[half].start()

    loads[4].wait()
    for half in range(2):
        shape = (HALF, LOCAL)
        pick = lax.broadcasted_iota(jnp.int32, shape, 1) == (
            2 * lax.broadcasted_iota(jnp.int32, shape, 0) + half
        )
        pick = pick.astype(jnp.float32).astype(jnp.bfloat16)
        for part in range(2):
            gain[half, part] = dot(pick, gain_in[part])

    def beam_rows(i, carry):
        cell = cell_ref[pl.ds(i, 1), :]
        x, y = cell // GRID_Y, cell % GRID_Y
        rows = pl.ds(pl.multiple_of(i * 128, 128), 128)
        y_column = column(y.astype(jnp.float32))
        lanes = lax.broadcasted_iota(jnp.int32, (128, GRID_Y), 1).astype(jnp.float32)
        hot = (lanes == y_column).astype(jnp.float32).astype(jnp.bfloat16)
        both = dot(hot, row_ref[...])
        cos, sin = both[:, :GRID_Y], both[:, GRID_Y:]
        for u in range(GRID_X):
            turn = column(((u * x) % 4).astype(jnp.float32))
            real = jnp.where(turn == 0, cos, jnp.where(turn == 1, -sin, jnp.where(turn == 2, -cos, sin)))
            imag = jnp.where(turn == 0, -sin, jnp.where(turn == 1, -cos, jnp.where(turn == 2, sin, cos)))
            beam_tab[0, rows, u * GRID_Y : (u + 1) * GRID_Y] = real.astype(jnp.bfloat16)
            beam_tab[1, rows, u * GRID_Y : (u + 1) * GRID_Y] = imag.astype(jnp.bfloat16)
        return carry

    lax.fori_loop(0, 8, beam_rows, 0)

    for load in loads[5:]:
        load.wait()
    for half in range(2):

        def phases(i, carry):
            tile, block = i // 8, i % 8
            step = delay[tile, pl.ds(half + 128 * block, 64, stride=2), :] & (TDFT - 1)
            rows = pl.ds(pl.multiple_of(half * 512 + block * 64, 64), 64)
            lanes = pl.ds(pl.multiple_of(tile * 128, 128), 128)
            sign = (1 - 2 * (step & 1)).astype(jnp.float32)
            cos, sin = cosine_of(step), cosine_of((step + 12) & (TDFT - 1))
            twice = 2.0 * cos
            cos_now, sin_now = cos, sin
            cos_last, sin_last = jnp.ones_like(cos), jnp.zeros_like(cos)
            for f in range(1, 5):
                phase[f - 1, 0, rows, lanes] = cos_now.astype(jnp.bfloat16)
                phase[f - 1, 1, rows, lanes] = sin_now.astype(jnp.bfloat16)
                if f < 4:
                    phase[7 - f, 0, rows, lanes] = (sign * cos_now).astype(jnp.bfloat16)
                    phase[7 - f, 1, rows, lanes] = (-sign * sin_now).astype(jnp.bfloat16)
                    cos_now, cos_last = twice * cos_now - cos_last, cos_now
                    sin_now, sin_last = twice * sin_now - sin_last, sin_now
            return carry

        lax.fori_loop(0, 32, phases, 0)

    offset = frame_matrix().sum(0)

    def calibrate(half, octet):
        feeds = pl.ds(pl.multiple_of(octet * 128, 128), 128)
        gain_real, gain_imag = gain[half, 0, :, feeds], gain[half, 1, :, feeds]

        def one(tile, total):
            lanes = pl.ds(pl.multiple_of(tile * 128, 128), 128)
            parts = [recv[half, octet * 8 + s, :, lanes].astype(jnp.float32) for s in range(8)]
            parts = exchange(parts)
            for n in range(0, 8, 2):
                reals, imags = [], []
                for part in parts[n : n + 2]:
                    real, imag = part[:HALF], part[HALF:]
                    reals.append(gain_real * real - gain_imag * imag)
                    imags.append(gain_real * imag + gain_imag * real)
                rows = pl.ds(pl.multiple_of(tile * 64 + n * HALF, LOCAL), LOCAL)
                for which, values in enumerate((reals, imags)):
                    value = jnp.concatenate(values, 0).astype(jnp.bfloat16)
                    cal[which, rows, feeds] = value
                    wide = value.astype(jnp.float32)
                    total = total + wide * wide
            return total

        return lax.fori_loop(0, 4, one, jnp.zeros((LOCAL, 128), jnp.float32))

    def arrive(half, octet, count):
        pltpu.make_async_remote_copy(
            recv.at[half, pl.ds(0, count)], recv.at[half, pl.ds(0, count)],
            send_sem.at[half], recv_sem.at[half, octet],
            device_id={"shard": me}, device_id_type=MESH,
        ).wait_recv()

    def level_copy(half, i):
        return pltpu.make_async_remote_copy(
            level_send.at[half], level_recv.at[half, place], level_send_sem.at[half, i - 1],
            level_recv_sem.at[half, place],
            device_id={"section": (place + i) % BLOCKS}, device_id_type=MESH,
        )

    def two_copy(half, dest):
        return pltpu.make_async_remote_copy(
            send_two.at[half, dest], recv_two.at[half, me], send_two_sem.at[half], recv_two_sem.at[half],
            device_id={"shard": dest}, device_id_type=MESH,
        )

    own_two = [
        pltpu.make_async_copy(send_two.at[half, me], recv_two.at[half, me], own_sem.at[2 + half])
        for half in range(2)
    ]

    for half in range(2):

        def octets(i, total):
            octet = plane_of(i)
            arrive(half, octet, 8)
            return total + calibrate(half, octet)

        total = lax.fori_loop(0, 7, octets, jnp.zeros((LOCAL, 128), jnp.float32))
        arrive(half, my_z, 7)
        own[half].wait()
        total = total + calibrate(half, my_z)
        total = jnp.sum(total[:HALF] + total[HALF:], axis=1, keepdims=True) * (1.0 / TDFT) + 1e-06
        level_send[half] = jnp.broadcast_to(total, (HALF, 128))
        level_recv[half, place] = jnp.broadcast_to(total, (HALF, 128))

        decay_row = jnp.broadcast_to(decay_ref[...], (HALF, LOCAL))
        pick = lax.broadcasted_iota(jnp.int32, (HALF, LOCAL), 1) == (
            2 * lax.broadcasted_iota(jnp.int32, (HALF, LOCAL), 0) + half
        )
        decay = jnp.sum(jnp.where(pick, decay_row, 0.0), axis=1, keepdims=True)
        decay = jnp.broadcast_to(decay, (HALF, 128))

        def beams(i, carry):
            wide = pl.ds(pl.multiple_of(i * 256, 256), 256)
            real_tab, imag_tab = beam_tab[0, :, wide], beam_tab[1, :, wide]
            real = dot(cal[0], real_tab) - dot(cal[1], imag_tab)
            imag = dot(cal[0], imag_tab) + dot(cal[1], real_tab)
            both = real * real + imag * imag
            power[i] = both[:128] + both[128:]

            return carry

        for i in range(1, BLOCKS):
            level_copy(half, i).start()
        lax.fori_loop(0, 4, beams, 0)
        for i in range(1, BLOCKS):
            other = (place + i) % BLOCKS
            pltpu.make_async_remote_copy(
                level_send.at[half], level_recv.at[half, other], level_send_sem.at[half, i - 1],
                level_recv_sem.at[half, other],
                device_id={"section": other}, device_id_type=MESH,
            ).wait_recv()
        dividend = jnp.zeros((HALF, 128), jnp.float32)
        divisor = jnp.zeros((HALF, 128), jnp.float32)
        for block in range(BLOCKS):
            use = block <= place
            dividend = jnp.where(use, decay * dividend + level_recv[half, block], dividend)
            divisor = jnp.where(use, decay * divisor + 1.0, divisor)
        scale = divisor / dividend

        def modulate(i, carry):
            for tile in range(2):
                lanes = slice(tile * 128, (tile + 1) * 128)
                frames = [power[i, n * HALF : (n + 1) * HALF, lanes] for n in range(TDFT)]
                freqs = frame_transform(frames)
                freqs = [v * scale - np.float32(offset[q]) for q, v in enumerate(freqs)]
                freqs = freqs + [jnp.zeros_like(scale)] * 2
                first, second = exchange(freqs[:8]), exchange(freqs[8:])
                for j in range(8):
                    both = jnp.concatenate([first[j], second[j]], 0)
                    send_two[half, i * 16 + tile * 8 + j] = both.astype(jnp.bfloat16)
            return carry

        lax.fori_loop(0, 4, modulate, 0)

        def send_rest(i, carry):
            two_copy(half, (me + i) % SHARDS).start()
            return carry

        lax.fori_loop(1, SHARDS, send_rest, 0)
        own_two[half].start()

    for half in range(2):
        pltpu.make_async_remote_copy(
            recv_two.at[half, pl.ds(0, SHARDS - 1)], recv_two.at[half, pl.ds(0, SHARDS - 1)],
            send_two_sem.at[half], recv_two_sem.at[half],
            device_id={"shard": me}, device_id_type=MESH,
        ).wait_recv()
        own_two[half].wait()
        data = recv_two[half].astype(jnp.float32)
        for group in range(2):
            rows = data[:, group * HALF : (group + 1) * HALF, :].reshape(SHARDS * HALF, 128)
            turned[group * 128 : (group + 1) * 128, :] = rows.T.astype(jnp.bfloat16)

        def dedisperse(f, carry):
            real = turned[pl.ds(pl.multiple_of(f * LOCAL, LOCAL), LOCAL), :]
            imag = turned[pl.ds(pl.multiple_of((f + MODF) * LOCAL, LOCAL), LOCAL), :]
            rows = slice(half * 512, (half + 1) * 512)
            total = dot(jnp.concatenate([real, imag], 0), phase[f, 0, rows, :])
            total = total + dot(jnp.concatenate([imag, -real], 0), phase[f, 1, rows, :])
            if half == 0:
                total_ref[f] = total
            else:
                total = total + total_ref[f]
                out_ref[f] = (total * (1.0 / math.sqrt(CHANS))).astype(jnp.bfloat16)
            return carry

        lax.fori_loop(0, MODF, dedisperse, 0)

    for half in range(2):
        pltpu.make_async_remote_copy(
            send.at[half, pl.ds(0, SHARDS - 1)], recv.at[half, pl.ds(0, SHARDS - 1)],
            send_sem.at[half], recv_sem.at[half, 0],
            device_id={"shard": me}, device_id_type=MESH,
        ).wait_send()
        pltpu.make_async_remote_copy(
            send_two.at[half, pl.ds(0, SHARDS - 1)], recv_two.at[half, pl.ds(0, SHARDS - 1)],
            send_two_sem.at[half], recv_two_sem.at[half],
            device_id={"shard": me}, device_id_type=MESH,
        ).wait_send()
        for i in range(1, BLOCKS):
            level_copy(half, i).wait_send()


def shards(voltages, feed_gains, grid_index, decay_rates, delays):
    bf16, f32 = jnp.bfloat16, jnp.float32
    anywhere = pl.BlockSpec(memory_space=pl.ANY)
    here = pl.BlockSpec(memory_space=pltpu.VMEM)
    dma = pltpu.SemaphoreType.DMA
    out = pl.pallas_call(
        body,
        out_shape=jax.ShapeDtypeStruct((MODF, 2 * LOCAL, TRIALS), bf16),
        in_specs=[anywhere] * 4 + [here] * 3,
        out_specs=here,
        scratch_shapes=[
            pltpu.VMEM((POL, LOCAL, TDFT * NSAMP), bf16),
            pltpu.VMEM((2, CHANS, FOLD), bf16),
            pltpu.VMEM((2, LOCAL, FEEDS), bf16),
            pltpu.VMEM((4, CHANS, 128), jnp.int32),
            pltpu.VMEM((2, ROWS, FOLD), bf16),
            pltpu.VMEM((2, SHARDS, LOCAL, ROWS), bf16),
            pltpu.VMEM((2, SHARDS, LOCAL, ROWS), bf16),
            pltpu.VMEM((2, 2, HALF, FEEDS), f32),
            pltpu.VMEM((2, ROWS // 2, FEEDS), bf16),
            pltpu.VMEM((2, FEEDS, FEEDS), bf16),
            pltpu.VMEM((MODF, 2, CHANS, TRIALS), bf16),
            pltpu.VMEM((4, TDFT * HALF, 256), f32),
            pltpu.VMEM((2, SHARDS, LOCAL, 128), bf16),
            pltpu.VMEM((2, SHARDS, LOCAL, 128), bf16),
            pltpu.VMEM((256, SHARDS * HALF), bf16),
            pltpu.VMEM((MODF, 2 * LOCAL, TRIALS), f32),
            pltpu.VMEM((2, HALF, 128), f32),
            pltpu.VMEM((2, BLOCKS, HALF, 128), f32),
            dma((9,)), dma((4,)), dma((2,)), dma((2, 8)), dma((2,)), dma((2,)),
            dma((2, BLOCKS - 1)), dma((2, BLOCKS)),
        ],
        compiler_params=pltpu.CompilerParams(
            collective_id=0, has_side_effects=True, vmem_limit_bytes=VMEM_LIMIT
        ),
        name="telescope",
    )(
        voltages[0], spectral_constant(), feed_gains, delays,
        grid_index.reshape(8, 128), decay_rates.reshape(1, LOCAL), row_constant(),
    )
    return out.reshape(MODF, 2, LOCAL, TRIALS).transpose(0, 3, 1, 2)[None]


def solution(mesh):
    in_specs = (P("section", None, "shard", None), P(None, "shard", None), P(), P("shard"), P())
    out_specs = P("section", None, None, None, "shard")
    return jax.shard_map(shards, mesh=mesh, in_specs=in_specs, out_specs=out_specs, check_vma=False)
```

```python
import math

import jax
import jax.numpy as jnp
import numpy as np
from jax import lax
from jax.experimental import pallas as pl
from jax.experimental.pallas import tpu as pltpu
from jax.sharding import PartitionSpec as P

POL = 2
GRID_X = 4
GRID_Y = 256
NSAMP = 2048
TDFT = 16
TRIALS = 512
FEEDS = 1024
CHANS = 1024
MODF = 7
BLOCKS = 4
SHARDS = 64
LOCAL = 16
QUARTER = LOCAL // 4
PIECES = 4
CLASSES = (0, 2, 1, 3)
ROWS = POL * TDFT * LOCAL
PIECE = SHARDS * 2 * QUARTER
VMEM_LIMIT = 62 * 1024 * 1024
MESH = pl.DeviceIdType.MESH


def spectral_constant(classes, length):
    shape = (len(classes), SHARDS, 2, QUARTER)
    which, dest, part, chan = np.meshgrid(*[np.arange(n) for n in shape], indexing="ij")
    chans = (dest * LOCAL + 4 * chan + np.asarray(classes)[which])[..., None].astype(np.int64)
    cols = np.arange(length, dtype=np.int64)
    angles = np.float32(2.0 * math.pi / NSAMP) * (chans * cols % NSAMP).astype(np.float32)
    table = np.where(part[..., None] == 0, np.cos(angles), -np.sin(angles)).astype(np.float32)
    return jnp.asarray(table.reshape(len(classes), PIECE, length)).astype(jnp.bfloat16)


def row_constant():
    rows = np.arange(GRID_Y)[:, None]
    cols = np.arange(GRID_Y)[None, :]
    angles = np.float32(2.0 * math.pi / GRID_Y) * (rows * cols % GRID_Y).astype(np.float32)
    table = np.concatenate([np.cos(angles), np.sin(angles)], 1).astype(np.float32)
    return jnp.asarray(table).astype(jnp.bfloat16)


def frame_matrix():
    frames = np.arange(TDFT)[:, None]
    freqs = np.arange(1, MODF + 1)[None, :]
    angles = 2.0 * math.pi / TDFT * (frames * freqs % TDFT)
    return np.concatenate([np.cos(angles), -np.sin(angles)], 1) / math.sqrt(TDFT)


def cosine_of(step):
    fold = jnp.abs(8 - step)
    out = jnp.full(step.shape, -math.cos(0.0), jnp.float32)
    for entry in range(1, 9):
        out = jnp.where(fold == entry, np.float32(-math.cos(2.0 * math.pi * entry / TDFT)), out)
    return out


def exchange(parts):
    parts = list(parts)
    lane = lax.broadcasted_iota(jnp.int32, parts[0].shape, 1)
    for bit in (4, 2, 1):
        upper = (lane & (bit * LOCAL)) != 0
        for i in range(8):
            if i & bit:
                continue
            low, high = parts[i], parts[i + bit]
            parts[i] = jnp.where(upper, pltpu.roll(high, bit * LOCAL, 1), low)
            parts[i + bit] = jnp.where(upper, high, pltpu.roll(low, 128 - bit * LOCAL, 1))
    return parts


def dot(a, b):
    return jnp.dot(a, b, preferred_element_type=jnp.float32)


def column(row):
    shape = (128, 128)
    same = lax.broadcasted_iota(jnp.int32, shape, 0) == lax.broadcasted_iota(jnp.int32, shape, 1)
    return jnp.sum(jnp.where(same, jnp.broadcast_to(row, shape), 0.0), axis=1, keepdims=True)


def body(
    volts_hbm, even_hbm, odd_hbm, gain_hbm, delay_hbm, cell_ref, decay_ref, row_ref, out_ref,
    volts, even, odd, gain_in, delay, fold_even, fold_odd, send, recv, gain, cal, beam_tab, phase, power,
    send_two, recv_two, turned, total_ref, level_send, level_recv,
    load_sem, own_sem, send_sem, recv_sem, send_two_sem, recv_two_sem, level_send_sem, level_recv_sem,
):
    f32, bf16 = jnp.float32, jnp.bfloat16
    me = lax.axis_index("shard")
    place = lax.axis_index("section")
    my_z, low = me // 8, me % 8

    load_volts = [
        pltpu.make_async_copy(volts_hbm.at[pol], volts.at[pol], load_sem.at[pol]) for pol in range(POL)
    ]
    load_even = [
        pltpu.make_async_copy(even_hbm.at[c], even.at[c], load_sem.at[2 + c]) for c in range(2)
    ]
    load_odd = [
        pltpu.make_async_copy(odd_hbm.at[c], odd.at[c], load_sem.at[4 + c]) for c in range(2)
    ]
    load_gain = pltpu.make_async_copy(gain_hbm, gain_in, load_sem.at[6])
    load_delay = [
        pltpu.make_async_copy(
            delay_hbm.at[:, pl.ds(tile * 128, 128)], delay.at[tile], load_sem.at[7 + tile]
        )
        for tile in range(4)
    ]
    for load in load_volts + load_even + load_odd + [load_gain] + load_delay:
        load.start()

    barrier = pltpu.get_barrier_semaphore()

    def greet(i, carry):
        pl.semaphore_signal(barrier, inc=1, device_id={"shard": (me + i) % SHARDS}, device_id_type=MESH)
        return carry

    lax.fori_loop(1, SHARDS, greet, 0)
    for i in range(1, BLOCKS):
        pl.semaphore_signal(
            barrier, inc=1, device_id={"section": (place + i) % BLOCKS}, device_id_type=MESH
        )

    def quarters(pol, frame):
        parts = []
        for s in range(4):
            lanes = pl.ds(pl.multiple_of(frame * NSAMP + s * 512, 512), 512)
            parts.append(volts[pol, :, lanes].astype(f32))
        return parts, pl.ds(pl.multiple_of((pol * TDFT + frame) * LOCAL, LOCAL), LOCAL)

    def fold_sum(pol):
        def one(frame, carry):
            (a, b, c, d), rows = quarters(pol, frame)
            fold_even[0, rows, :] = ((a + c) + (b + d)).astype(bf16)
            fold_even[1, rows, :] = ((a + c) - (b + d)).astype(bf16)
            return carry

        lax.fori_loop(0, TDFT, one, 0)

    def fold_difference(pol):
        def one(frame, carry):
            (a, b, c, d), rows = quarters(pol, frame)
            fold_odd[rows, :512] = (a - c).astype(bf16)
            fold_odd[rows, 512:] = (b - d).astype(bf16)
            return carry

        lax.fori_loop(0, TDFT, one, 0)

    def plane_of(i):
        step, side = i // 2, i % 2
        return (my_z + 4 + step - side * (2 * step + 1) + 8) % 8

    def send_one(piece, dest):
        pltpu.make_async_remote_copy(
            send.at[piece, dest], recv.at[piece, me], send_sem.at[piece], recv_sem.at[piece, my_z],
            device_id={"shard": dest}, device_id_type=MESH,
        ).start()

    def send_plane(piece, i):
        z = plane_of(i)

        def one(r, carry):
            send_one(piece, z * 8 + (low + r) % 8)
            return carry

        lax.fori_loop(0, 8, one, 0)

    own = [
        pltpu.make_async_copy(send.at[piece, me], recv.at[piece, me], own_sem.at[piece])
        for piece in range(PIECES)
    ]

    def channelize(piece):
        def block(i, carry):
            z = (my_z // 2 + 2 + i) % 4
            rows = pl.ds(pl.multiple_of(z * 128, 128), 128)
            table, data = (even[piece, rows, :], fold_even[piece]) if piece < 2 else (
                odd[piece - 2, rows, :], fold_odd[...]
            )
            spectra = lax.dot_general(
                table, data, (((1,), (1,)), ((), ())), preferred_element_type=f32
            )
            spectra = (spectra * (1.0 / math.sqrt(NSAMP))).reshape(16, 8, ROWS)
            both = jnp.concatenate([spectra[:, :, : ROWS // 2], spectra[:, :, ROWS // 2 :]], 1)
            send[piece, pl.ds(pl.multiple_of(z * 16, 16), 16)] = both.astype(bf16)
            return carry

        lax.fori_loop(0, 4, block, 0)

    def send_piece(piece):
        def plane(i, carry):
            send_plane(piece, i)
            return carry

        lax.fori_loop(0, 7, plane, 0)

        def last(r, carry):
            send_one(piece, my_z * 8 + (low + r) % 8)
            return carry

        lax.fori_loop(1, 8, last, 0)
        own[piece].start()

    for pol in range(POL):
        load_volts[pol].wait()
        fold_sum(pol)
    load_even[0].wait()
    channelize(0)
    pl.semaphore_wait(barrier, SHARDS - 1 + BLOCKS - 1)
    send_piece(0)
    load_even[1].wait()
    channelize(1)
    send_piece(1)
    for pol in range(POL):
        fold_difference(pol)
    for piece in (2, 3):
        load_odd[piece - 2].wait()
        channelize(piece)
        send_piece(piece)

    def chan_pick(piece):
        shape = (8, LOCAL)
        row = lax.broadcasted_iota(jnp.int32, shape, 0) % QUARTER
        return lax.broadcasted_iota(jnp.int32, shape, 1) == 4 * row + CLASSES[piece]

    lower = lax.broadcasted_iota(jnp.int32, (8, 128), 0) < QUARTER
    sign = jnp.where(lower, -1.0, 1.0).astype(f32)

    load_gain.wait()
    for piece in range(PIECES):
        pick = chan_pick(piece).astype(f32).astype(bf16)
        gain[piece, 0] = dot(pick, gain_in[0])
        gain[piece, 1] = dot(pick, gain_in[1]) * sign[:, :1]

    def beam_rows(i, carry):
        cell = cell_ref[pl.ds(i, 1), :]
        x, y = cell // GRID_Y, cell % GRID_Y
        rows = pl.ds(pl.multiple_of(i * 128, 128), 128)
        y_column = column(y.astype(f32))
        lanes = lax.broadcasted_iota(jnp.int32, (128, GRID_Y), 1).astype(f32)
        hot = (lanes == y_column).astype(f32).astype(bf16)
        both = dot(hot, row_ref[...])
        cos, sin = both[:, :GRID_Y], both[:, GRID_Y:]
        for u in range(GRID_X):
            turn = column(((u * x) % 4).astype(f32))
            real = jnp.where(turn == 0, cos, jnp.where(turn == 1, -sin, jnp.where(turn == 2, -cos, sin)))
            imag = jnp.where(turn == 0, -sin, jnp.where(turn == 1, -cos, jnp.where(turn == 2, sin, cos)))
            beam_tab[0, rows, u * GRID_Y : (u + 1) * GRID_Y] = real.astype(bf16)
            beam_tab[1, rows, u * GRID_Y : (u + 1) * GRID_Y] = imag.astype(bf16)
        return carry

    lax.fori_loop(0, 8, beam_rows, 0)

    for load in load_delay:
        load.wait()
    for piece in range(PIECES):

        def phases(i, carry):
            tile, block = i // 4, i % 4
            step = delay[tile, pl.ds(CLASSES[piece] + 256 * block, 64, stride=4), :] & (TDFT - 1)
            rows = pl.ds(pl.multiple_of(piece * 256 + block * 64, 64), 64)
            lanes = pl.ds(pl.multiple_of(tile * 128, 128), 128)
            parity = (1 - 2 * (step & 1)).astype(f32)
            cos, sin = cosine_of(step), cosine_of((step + 12) & (TDFT - 1))
            twice = 2.0 * cos
            cos_now, sin_now = cos, sin
            cos_last, sin_last = jnp.ones_like(cos), jnp.zeros_like(cos)
            for f in range(1, 5):
                phase[f - 1, 0, rows, lanes] = cos_now.astype(bf16)
                phase[f - 1, 1, rows, lanes] = sin_now.astype(bf16)
                if f < 4:
                    phase[7 - f, 0, rows, lanes] = (parity * cos_now).astype(bf16)
                    phase[7 - f, 1, rows, lanes] = (-parity * sin_now).astype(bf16)
                    cos_now, cos_last = twice * cos_now - cos_last, cos_now
                    sin_now, sin_last = twice * sin_now - sin_last, sin_now
            return carry

        lax.fori_loop(0, 16, phases, 0)

    def calibrate(piece, octet):
        feeds = pl.ds(pl.multiple_of(octet * 128, 128), 128)
        straight, crossed = gain[piece, 0, :, feeds], gain[piece, 1, :, feeds]

        def one(tile, total):
            lanes = pl.ds(pl.multiple_of(tile * 128, 128), 128)
            parts = [recv[piece, octet * 8 + s, :, lanes].astype(f32) for s in range(8)]
            parts = exchange(parts)
            for pol in range(POL):
                values = []
                for part in parts:
                    value = part[pol * 8 : pol * 8 + 8]
                    values.append(straight * value + crossed * pltpu.roll(value, QUARTER, 0))
                for n in range(0, 8, 2):
                    rows = pl.ds(pl.multiple_of(pol * 128 + tile * 64 + n * 8, LOCAL), LOCAL)
                    value = jnp.concatenate(values[n : n + 2], 0).astype(bf16)
                    cal[rows, feeds] = value
                    wide = value.astype(f32)
                    total = total + wide * wide
            return total

        return lax.fori_loop(0, 2, one, jnp.zeros((LOCAL, 128), f32))

    def arrive(piece, octet, count):
        pltpu.make_async_remote_copy(
            recv.at[piece, pl.ds(0, count)], recv.at[piece, pl.ds(0, count)],
            send_sem.at[piece], recv_sem.at[piece, octet],
            device_id={"shard": me}, device_id_type=MESH,
        ).wait_recv()

    def level_copy(piece, i):
        return pltpu.make_async_remote_copy(
            level_send.at[piece], level_recv.at[piece, place], level_send_sem.at[piece, i - 1],
            level_recv_sem.at[piece, place],
            device_id={"section": (place + i) % BLOCKS}, device_id_type=MESH,
        )

    def send_two_one(piece, dest):
        pltpu.make_async_remote_copy(
            send_two.at[piece, dest], recv_two.at[piece, me], send_two_sem.at[piece],
            recv_two_sem.at[piece], device_id={"shard": dest}, device_id_type=MESH,
        ).start()

    own_two = [
        pltpu.make_async_copy(
            send_two.at[piece, me], recv_two.at[piece, me], own_sem.at[PIECES + piece]
        )
        for piece in range(PIECES)
    ]
    factors = frame_matrix()
    evens = [1, 3, 5, 1 + MODF, 3 + MODF, 5 + MODF, None, None]
    odds = [0, 2, 4, 6, MODF, 2 + MODF, 4 + MODF, 6 + MODF]

    def pair(first, second):
        return jnp.where(lower, np.float32(first), np.float32(second))

    for piece in range(PIECES):

        def octets(i, total):
            octet = plane_of(i)
            arrive(piece, octet, 8)
            return total + calibrate(piece, octet)

        total = lax.fori_loop(0, 7, octets, jnp.zeros((LOCAL, 128), f32))
        arrive(piece, my_z, 7)
        own[piece].wait()
        total = total + calibrate(piece, my_z)
        total = total[:8] + total[8:]
        total = total + pltpu.roll(total, QUARTER, 0)
        total = jnp.sum(total, axis=1, keepdims=True) * (1.0 / TDFT) + 1e-06
        level_send[piece] = jnp.broadcast_to(total, (8, 128))
        level_recv[piece, place] = jnp.broadcast_to(total, (8, 128))

        decay_row = jnp.broadcast_to(decay_ref[...], (8, LOCAL))
        decay = jnp.sum(jnp.where(chan_pick(piece), decay_row, 0.0), axis=1, keepdims=True)
        decay = jnp.broadcast_to(decay, (8, 128))

        def beams(i, carry):
            wide = pl.ds(pl.multiple_of(i * 256, 256), 256)
            straight = dot(cal[...], beam_tab[0, :, wide]).reshape(32, 8, 256)
            crossed = dot(cal[...], beam_tab[1, :, wide]).reshape(32, 8, 256)
            value = straight + pltpu.roll(crossed, QUARTER, 1) * sign[:, :1]
            value = value * value
            value = value[:TDFT] + value[TDFT:]
            power[i] = value + pltpu.roll(value, QUARTER, 1)
            return carry

        for i in range(1, BLOCKS):
            level_copy(piece, i).start()
        lax.fori_loop(0, 4, beams, 0)
        for i in range(1, BLOCKS):
            other = (place + i) % BLOCKS
            pltpu.make_async_remote_copy(
                level_send.at[piece], level_recv.at[piece, other], level_send_sem.at[piece, i - 1],
                level_recv_sem.at[piece, other],
                device_id={"section": other}, device_id_type=MESH,
            ).wait_recv()
        dividend = jnp.zeros((8, 128), f32)
        divisor = jnp.zeros((8, 128), f32)
        for block in range(BLOCKS):
            use = block <= place
            dividend = jnp.where(use, decay * dividend + level_recv[piece, block], dividend)
            divisor = jnp.where(use, decay * divisor + 1.0, divisor)
        scale = divisor / dividend

        def modulate(i, carry):
            for tile in range(2):
                lanes = slice(tile * 128, (tile + 1) * 128)
                frames = []
                for n in range(TDFT // 2):
                    later = power[i, n + TDFT // 2, :, lanes]
                    frames.append(power[i, n, :, lanes] - sign * later)
                freqs = []
                for q_even, q_odd in zip(evens, odds):
                    column_even = np.zeros(TDFT) if q_even is None else factors[:, q_even]
                    column_odd = factors[:, q_odd]
                    value = None
                    for n in range(TDFT // 2):
                        first, second = float(column_even[n]), float(column_odd[n])
                        if max(abs(first), abs(second)) < 1e-12:
                            continue
                        term = frames[n] * pair(first, second)
                        value = term if value is None else value + term
                    freqs.append(value * scale - pair(column_even.sum(), column_odd.sum()))
                for j, part in enumerate(exchange(freqs)):
                    send_two[piece, i * 16 + tile * 8 + j] = part.astype(bf16)
            return carry

        lax.fori_loop(0, 4, modulate, 0)

        def two_plane(i, carry):
            z = plane_of(i)

            def one(r, inner):
                send_two_one(piece, z * 8 + (low + r) % 8)
                return inner

            return lax.fori_loop(0, 8, one, carry)

        lax.fori_loop(0, 7, two_plane, 0)

        def two_last(r, carry):
            send_two_one(piece, my_z * 8 + (low + r) % 8)
            return carry

        lax.fori_loop(1, 8, two_last, 0)
        own_two[piece].start()

    for piece in range(PIECES):
        pltpu.make_async_remote_copy(
            recv_two.at[piece, pl.ds(0, SHARDS - 1)], recv_two.at[piece, pl.ds(0, SHARDS - 1)],
            send_two_sem.at[piece], recv_two_sem.at[piece],
            device_id={"shard": me}, device_id_type=MESH,
        ).wait_recv()
        own_two[piece].wait()
        data = recv_two[piece].astype(f32).reshape(SHARDS // 2, 2, 8, 128)
        first, second = data[:, 0], data[:, 1]
        mask = lower[None]
        split = (
            jnp.where(mask, first, pltpu.roll(second, QUARTER, 1)),
            jnp.where(mask, pltpu.roll(first, QUARTER, 1), second),
        )
        for side in range(2):
            turned[side] = split[side].reshape(SHARDS * QUARTER, 128).T.astype(bf16)

        def dedisperse(g, carry):
            side, at = (g + 1) % 2, g // 2
            real = turned[side, pl.ds(pl.multiple_of(at * LOCAL, LOCAL), LOCAL), :]
            imag = turned[side, pl.ds(pl.multiple_of((at + 3 + side) * LOCAL, LOCAL), LOCAL), :]
            rows = slice(piece * 256, (piece + 1) * 256)
            total = dot(jnp.concatenate([real, imag], 0), phase[g, 0, rows, :])
            total = total + dot(jnp.concatenate([imag, -real], 0), phase[g, 1, rows, :])
            if piece > 0:
                total = total + total_ref[g]
            if piece < PIECES - 1:
                total_ref[g] = total
            else:
                out_ref[g] = (total * (1.0 / math.sqrt(CHANS))).astype(bf16)
            return carry

        lax.fori_loop(0, MODF, dedisperse, 0)

    for piece in range(PIECES):
        pltpu.make_async_remote_copy(
            send.at[piece, pl.ds(0, SHARDS - 1)], recv.at[piece, pl.ds(0, SHARDS - 1)],
            send_sem.at[piece], recv_sem.at[piece, 0],
            device_id={"shard": me}, device_id_type=MESH,
        ).wait_send()
        pltpu.make_async_remote_copy(
            send_two.at[piece, pl.ds(0, SHARDS - 1)], recv_two.at[piece, pl.ds(0, SHARDS - 1)],
            send_two_sem.at[piece], recv_two_sem.at[piece],
            device_id={"shard": me}, device_id_type=MESH,
        ).wait_send()
        for i in range(1, BLOCKS):
            level_copy(piece, i).wait_send()


def shards(voltages, feed_gains, grid_index, decay_rates, delays):
    bf16, f32 = jnp.bfloat16, jnp.float32
    anywhere = pl.BlockSpec(memory_space=pl.ANY)
    here = pl.BlockSpec(memory_space=pltpu.VMEM)
    dma = pltpu.SemaphoreType.DMA
    out = pl.pallas_call(
        body,
        out_shape=jax.ShapeDtypeStruct((MODF, 2 * LOCAL, TRIALS), bf16),
        in_specs=[anywhere] * 5 + [here] * 3,
        out_specs=here,
        scratch_shapes=[
            pltpu.VMEM((POL, LOCAL, TDFT * NSAMP), bf16),
            pltpu.VMEM((2, PIECE, NSAMP // 4), bf16),
            pltpu.VMEM((2, PIECE, NSAMP // 2), bf16),
            pltpu.VMEM((2, LOCAL, FEEDS), bf16),
            pltpu.VMEM((4, CHANS, 128), jnp.int32),
            pltpu.VMEM((2, ROWS, NSAMP // 4), bf16),
            pltpu.VMEM((ROWS, NSAMP // 2), bf16),
            pltpu.VMEM((PIECES, SHARDS, LOCAL, ROWS // 2), bf16),
            pltpu.VMEM((PIECES, SHARDS, LOCAL, ROWS // 2), bf16),
            pltpu.VMEM((PIECES, 2, 8, FEEDS), f32),
            pltpu.VMEM((POL * TDFT * 8, FEEDS), bf16),
            pltpu.VMEM((2, FEEDS, FEEDS), bf16),
            pltpu.VMEM((MODF, 2, CHANS, TRIALS), bf16),
            pltpu.VMEM((4, TDFT, 8, 256), f32),
            pltpu.VMEM((PIECES, SHARDS, 8, 128), bf16),
            pltpu.VMEM((PIECES, SHARDS, 8, 128), bf16),
            pltpu.VMEM((2, 128, SHARDS * QUARTER), bf16),
            pltpu.VMEM((MODF, 2 * LOCAL, TRIALS), f32),
            pltpu.VMEM((PIECES, 8, 128), f32),
            pltpu.VMEM((PIECES, BLOCKS, 8, 128), f32),
            dma((11,)), dma((2 * PIECES,)), dma((PIECES,)), dma((PIECES, 8)), dma((PIECES,)),
            dma((PIECES,)), dma((PIECES, BLOCKS - 1)), dma((PIECES, BLOCKS)),
        ],
        compiler_params=pltpu.CompilerParams(
            collective_id=0, has_side_effects=True, vmem_limit_bytes=VMEM_LIMIT
        ),
        name="telescope",
    )(
        voltages[0], spectral_constant(CLASSES[:2], NSAMP // 4),
        spectral_constant(CLASSES[2:], NSAMP // 2), feed_gains, delays,
        grid_index.reshape(8, 128), decay_rates.reshape(1, LOCAL), row_constant(),
    )
    return out.reshape(MODF, 2, LOCAL, TRIALS).transpose(0, 3, 1, 2)[None]


def solution(mesh):
    in_specs = (P("section", None, "shard", None), P(None, "shard", None), P(), P("shard"), P())
    out_specs = P("section", None, None, None, "shard")
    return jax.shard_map(shards, mesh=mesh, in_specs=in_specs, out_specs=out_specs, check_vma=False)
```

```python
import math

import jax
import jax.numpy as jnp
import numpy as np
from jax import lax
from jax.experimental import pallas as pl
from jax.experimental.pallas import tpu as pltpu
from jax.sharding import PartitionSpec as P

POL = 2
GRID_X = 4
GRID_Y = 256
NSAMP = 2048
TDFT = 16
TRIALS = 512
FEEDS = 1024
CHANS = 1024
MODF = 7
BLOCKS = 4
SHARDS = 64
LOCAL = 16
QUARTER = LOCAL // 4
PIECES = 4
CLASSES = (0, 2, 1, 3)
ROWS = POL * TDFT * LOCAL
PIECE = SHARDS * 2 * QUARTER
VMEM_LIMIT = 62 * 1024 * 1024
MESH = pl.DeviceIdType.MESH


def spectral_constant(classes, length):
    shape = (len(classes), SHARDS, 2, QUARTER)
    which, dest, part, chan = np.meshgrid(*[np.arange(n) for n in shape], indexing="ij")
    chans = (dest * LOCAL + 4 * chan + np.asarray(classes)[which])[..., None].astype(np.int64)
    cols = np.arange(length, dtype=np.int64)
    angles = np.float32(2.0 * math.pi / NSAMP) * (chans * cols % NSAMP).astype(np.float32)
    table = np.where(part[..., None] == 0, np.cos(angles), -np.sin(angles)).astype(np.float32)
    return jnp.asarray(table.reshape(len(classes), PIECE, length)).astype(jnp.bfloat16)


def row_constant():
    rows = np.arange(GRID_Y)[:, None]
    cols = np.arange(GRID_Y)[None, :]
    angles = np.float32(2.0 * math.pi / GRID_Y) * (rows * cols % GRID_Y).astype(np.float32)
    table = np.concatenate([np.cos(angles), np.sin(angles)], 1).astype(np.float32)
    return jnp.asarray(table).astype(jnp.bfloat16)


def frame_matrix():
    frames = np.arange(TDFT)[:, None]
    freqs = np.arange(1, MODF + 1)[None, :]
    angles = 2.0 * math.pi / TDFT * (frames * freqs % TDFT)
    return np.concatenate([np.cos(angles), -np.sin(angles)], 1) / math.sqrt(TDFT)


def cosine_of(step):
    fold = jnp.abs(8 - step)
    out = jnp.full(step.shape, -math.cos(0.0), jnp.float32)
    for entry in range(1, 9):
        out = jnp.where(fold == entry, np.float32(-math.cos(2.0 * math.pi * entry / TDFT)), out)
    return out


def exchange(parts):
    parts = list(parts)
    lane = lax.broadcasted_iota(jnp.int32, parts[0].shape, 1)
    for bit in (4, 2, 1):
        upper = (lane & (bit * LOCAL)) != 0
        for i in range(8):
            if i & bit:
                continue
            low, high = parts[i], parts[i + bit]
            parts[i] = jnp.where(upper, pltpu.roll(high, bit * LOCAL, 1), low)
            parts[i + bit] = jnp.where(upper, high, pltpu.roll(low, 128 - bit * LOCAL, 1))
    return parts


def dot(a, b):
    return jnp.dot(a, b, preferred_element_type=jnp.float32)


def column(row):
    shape = (128, 128)
    same = lax.broadcasted_iota(jnp.int32, shape, 0) == lax.broadcasted_iota(jnp.int32, shape, 1)
    return jnp.sum(jnp.where(same, jnp.broadcast_to(row, shape), 0.0), axis=1, keepdims=True)


def body(
    volts_hbm, even_hbm, odd_hbm, gain_hbm, delay_hbm, cell_hbm, decay_hbm, row_hbm, out_ref,
    volts, even, odd, gain_in, delay, cell_ref, decay_ref, row_ref, fold_even, fold_odd, send, recv, gain, cal, beam_tab, phase, power,
    send_two, recv_two, turned, total_ref, level_send, level_recv,
    load_sem, own_sem, send_sem, recv_sem, send_two_sem, recv_two_sem, level_send_sem, level_recv_sem,
):
    f32, bf16 = jnp.float32, jnp.bfloat16
    me = lax.axis_index("shard")
    place = lax.axis_index("section")
    my_z, low = me // 8, me % 8

    load_volts = [
        pltpu.make_async_copy(volts_hbm.at[pol], volts.at[pol], load_sem.at[pol]) for pol in range(POL)
    ]
    load_even = [
        pltpu.make_async_copy(even_hbm.at[c], even.at[c], load_sem.at[2 + c]) for c in range(2)
    ]
    load_odd = [
        pltpu.make_async_copy(odd_hbm.at[c], odd.at[c], load_sem.at[4 + c]) for c in range(2)
    ]
    load_gain = pltpu.make_async_copy(gain_hbm, gain_in, load_sem.at[6])
    load_delay = [
        pltpu.make_async_copy(
            delay_hbm.at[:, pl.ds(tile * 128, 128)], delay.at[tile], load_sem.at[7 + tile]
        )
        for tile in range(4)
    ]
    load_small = [
        pltpu.make_async_copy(cell_hbm, cell_ref, load_sem.at[11]),
        pltpu.make_async_copy(decay_hbm, decay_ref, load_sem.at[12]),
        pltpu.make_async_copy(row_hbm, row_ref, load_sem.at[13]),
    ]
    for load in load_volts + load_even[:1]:
        load.start()

    barrier = pltpu.get_barrier_semaphore()

    def greet(i, carry):
        pl.semaphore_signal(barrier, inc=1, device_id={"shard": (me + i) % SHARDS}, device_id_type=MESH)
        return carry

    lax.fori_loop(1, SHARDS, greet, 0)
    for i in range(1, BLOCKS):
        pl.semaphore_signal(
            barrier, inc=1, device_id={"section": (place + i) % BLOCKS}, device_id_type=MESH
        )

    def quarters(pol, frame):
        parts = []
        for s in range(4):
            lanes = pl.ds(pl.multiple_of(frame * NSAMP + s * 512, 512), 512)
            parts.append(volts[pol, :, lanes].astype(f32))
        return parts, pl.ds(pl.multiple_of((pol * TDFT + frame) * LOCAL, LOCAL), LOCAL)

    def fold_sum(pol):
        def one(frame, carry):
            (a, b, c, d), rows = quarters(pol, frame)
            fold_even[0, rows, :] = ((a + c) + (b + d)).astype(bf16)
            fold_even[1, rows, :] = ((a + c) - (b + d)).astype(bf16)
            return carry

        lax.fori_loop(0, TDFT, one, 0)

    def fold_difference(pol):
        def one(frame, carry):
            (a, b, c, d), rows = quarters(pol, frame)
            fold_odd[rows, :512] = (a - c).astype(bf16)
            fold_odd[rows, 512:] = (b - d).astype(bf16)
            return carry

        lax.fori_loop(0, TDFT, one, 0)

    def plane_of(i):
        step, side = i // 2, i % 2
        return (my_z + 4 + step - side * (2 * step + 1) + 8) % 8

    def send_one(piece, dest):
        pltpu.make_async_remote_copy(
            send.at[piece, dest], recv.at[piece, me], send_sem.at[piece], recv_sem.at[piece, my_z],
            device_id={"shard": dest}, device_id_type=MESH,
        ).start()

    def send_plane(piece, i):
        z = plane_of(i)

        def one(r, carry):
            send_one(piece, z * 8 + (low + r) % 8)
            return carry

        lax.fori_loop(0, 8, one, 0)

    own = [
        pltpu.make_async_copy(send.at[piece, me], recv.at[piece, me], own_sem.at[piece])
        for piece in range(PIECES)
    ]

    def channelize(piece):
        def block(i, carry):
            z = (my_z // 2 + 2 + i) % 4
            rows = pl.ds(pl.multiple_of(z * 128, 128), 128)
            table, data = (even[piece, rows, :], fold_even[piece]) if piece < 2 else (
                odd[piece - 2, rows, :], fold_odd[...]
            )
            spectra = lax.dot_general(
                table, data, (((1,), (1,)), ((), ())), preferred_element_type=f32
            )
            spectra = (spectra * (1.0 / math.sqrt(NSAMP))).reshape(16, 8, ROWS)
            both = jnp.concatenate([spectra[:, :, : ROWS // 2], spectra[:, :, ROWS // 2 :]], 1)
            send[piece, pl.ds(pl.multiple_of(z * 16, 16), 16)] = both.astype(bf16)
            return carry

        lax.fori_loop(0, 4, block, 0)

    def send_piece(piece):
        def plane(i, carry):
            send_plane(piece, i)
            return carry

        lax.fori_loop(0, 7, plane, 0)

        def last(r, carry):
            send_one(piece, my_z * 8 + (low + r) % 8)
            return carry

        lax.fori_loop(1, 8, last, 0)
        own[piece].start()

    for pol in range(POL):
        load_volts[pol].wait()
        fold_sum(pol)
    load_even[0].wait()
    for load in load_even[1:] + load_odd + [load_gain] + load_small + load_delay:
        load.start()
    channelize(0)
    pl.semaphore_wait(barrier, SHARDS - 1 + BLOCKS - 1)
    send_piece(0)
    load_even[1].wait()
    channelize(1)
    send_piece(1)
    for pol in range(POL):
        fold_difference(pol)
    for piece in (2, 3):
        load_odd[piece - 2].wait()
        channelize(piece)
        send_piece(piece)

    def chan_pick(piece):
        shape = (8, LOCAL)
        row = lax.broadcasted_iota(jnp.int32, shape, 0) % QUARTER
        return lax.broadcasted_iota(jnp.int32, shape, 1) == 4 * row + CLASSES[piece]

    lower = lax.broadcasted_iota(jnp.int32, (8, 128), 0) < QUARTER
    sign = jnp.where(lower, -1.0, 1.0).astype(f32)

    load_gain.wait()
    for load in load_small:
        load.wait()
    for piece in range(PIECES):
        pick = chan_pick(piece).astype(f32).astype(bf16)
        gain[piece, 0] = dot(pick, gain_in[0])
        gain[piece, 1] = dot(pick, gain_in[1]) * sign[:, :1]

    def beam_rows(i, carry):
        cell = cell_ref[pl.ds(i, 1), :]
        x, y = cell // GRID_Y, cell % GRID_Y
        rows = pl.ds(pl.multiple_of(i * 128, 128), 128)
        y_column = column(y.astype(f32))
        lanes = lax.broadcasted_iota(jnp.int32, (128, GRID_Y), 1).astype(f32)
        hot = (lanes == y_column).astype(f32).astype(bf16)
        both = dot(hot, row_ref[...])
        cos, sin = both[:, :GRID_Y], both[:, GRID_Y:]
        for u in range(GRID_X):
            turn = column(((u * x) % 4).astype(f32))
            real = jnp.where(turn == 0, cos, jnp.where(turn == 1, -sin, jnp.where(turn == 2, -cos, sin)))
            imag = jnp.where(turn == 0, -sin, jnp.where(turn == 1, -cos, jnp.where(turn == 2, sin, cos)))
            beam_tab[0, rows, u * GRID_Y : (u + 1) * GRID_Y] = real.astype(bf16)
            beam_tab[1, rows, u * GRID_Y : (u + 1) * GRID_Y] = imag.astype(bf16)
        return carry

    lax.fori_loop(0, 8, beam_rows, 0)

    for load in load_delay:
        load.wait()
    for piece in range(PIECES):

        def phases(i, carry):
            tile, block = i // 4, i % 4
            step = delay[tile, pl.ds(CLASSES[piece] + 256 * block, 64, stride=4), :] & (TDFT - 1)
            rows = pl.ds(pl.multiple_of(piece * 256 + block * 64, 64), 64)
            lanes = pl.ds(pl.multiple_of(tile * 128, 128), 128)
            parity = (1 - 2 * (step & 1)).astype(f32)
            cos, sin = cosine_of(step), cosine_of((step + 12) & (TDFT - 1))
            twice = 2.0 * cos
            cos_now, sin_now = cos, sin
            cos_last, sin_last = jnp.ones_like(cos), jnp.zeros_like(cos)
            for f in range(1, 5):
                phase[f - 1, 0, rows, lanes] = cos_now.astype(bf16)
                phase[f - 1, 1, rows, lanes] = sin_now.astype(bf16)
                if f < 4:
                    phase[7 - f, 0, rows, lanes] = (parity * cos_now).astype(bf16)
                    phase[7 - f, 1, rows, lanes] = (-parity * sin_now).astype(bf16)
                    cos_now, cos_last = twice * cos_now - cos_last, cos_now
                    sin_now, sin_last = twice * sin_now - sin_last, sin_now
            return carry

        lax.fori_loop(0, 16, phases, 0)

    def calibrate(piece, octet):
        feeds = pl.ds(pl.multiple_of(octet * 128, 128), 128)
        straight, crossed = gain[piece, 0, :, feeds], gain[piece, 1, :, feeds]

        def one(tile, total):
            lanes = pl.ds(pl.multiple_of(tile * 128, 128), 128)
            parts = [recv[piece, octet * 8 + s, :, lanes].astype(f32) for s in range(8)]
            parts = exchange(parts)
            for pol in range(POL):
                values = []
                for part in parts:
                    value = part[pol * 8 : pol * 8 + 8]
                    values.append(straight * value + crossed * pltpu.roll(value, QUARTER, 0))
                for n in range(0, 8, 2):
                    rows = pl.ds(pl.multiple_of(pol * 128 + tile * 64 + n * 8, LOCAL), LOCAL)
                    value = jnp.concatenate(values[n : n + 2], 0).astype(bf16)
                    cal[rows, feeds] = value
                    wide = value.astype(f32)
                    total = total + wide * wide
            return total

        return lax.fori_loop(0, 2, one, jnp.zeros((LOCAL, 128), f32))

    def arrive(piece, octet, count):
        pltpu.make_async_remote_copy(
            recv.at[piece, pl.ds(0, count)], recv.at[piece, pl.ds(0, count)],
            send_sem.at[piece], recv_sem.at[piece, octet],
            device_id={"shard": me}, device_id_type=MESH,
        ).wait_recv()

    def level_copy(piece, i):
        return pltpu.make_async_remote_copy(
            level_send.at[piece], level_recv.at[piece, place], level_send_sem.at[piece, i - 1],
            level_recv_sem.at[piece, place],
            device_id={"section": (place + i) % BLOCKS}, device_id_type=MESH,
        )

    def send_two_one(piece, dest):
        pltpu.make_async_remote_copy(
            send_two.at[piece, dest], recv_two.at[piece, me], send_two_sem.at[piece],
            recv_two_sem.at[piece], device_id={"shard": dest}, device_id_type=MESH,
        ).start()

    own_two = [
        pltpu.make_async_copy(
            send_two.at[piece, me], recv_two.at[piece, me], own_sem.at[PIECES + piece]
        )
        for piece in range(PIECES)
    ]
    factors = frame_matrix()
    evens = [1, 3, 5, 1 + MODF, 3 + MODF, 5 + MODF, None, None]
    odds = [0, 2, 4, 6, MODF, 2 + MODF, 4 + MODF, 6 + MODF]

    def pair(first, second):
        return jnp.where(lower, np.float32(first), np.float32(second))

    for piece in range(PIECES):

        def octets(i, total):
            octet = plane_of(i)
            arrive(piece, octet, 8)
            return total + calibrate(piece, octet)

        total = lax.fori_loop(0, 7, octets, jnp.zeros((LOCAL, 128), f32))
        arrive(piece, my_z, 7)
        own[piece].wait()
        total = total + calibrate(piece, my_z)
        total = total[:8] + total[8:]
        total = total + pltpu.roll(total, QUARTER, 0)
        total = jnp.sum(total, axis=1, keepdims=True) * (1.0 / TDFT) + 1e-06
        level_send[piece] = jnp.broadcast_to(total, (8, 128))
        level_recv[piece, place] = jnp.broadcast_to(total, (8, 128))

        decay_row = jnp.broadcast_to(decay_ref[...], (8, LOCAL))
        decay = jnp.sum(jnp.where(chan_pick(piece), decay_row, 0.0), axis=1, keepdims=True)
        decay = jnp.broadcast_to(decay, (8, 128))

        def beams(i, carry):
            wide = pl.ds(pl.multiple_of(i * 256, 256), 256)
            straight = dot(cal[...], beam_tab[0, :, wide]).reshape(32, 8, 256)
            crossed = dot(cal[...], beam_tab[1, :, wide]).reshape(32, 8, 256)
            value = straight + pltpu.roll(crossed, QUARTER, 1) * sign[:, :1]
            value = value * value
            value = value[:TDFT] + value[TDFT:]
            power[i] = value + pltpu.roll(value, QUARTER, 1)
            return carry

        for i in range(1, BLOCKS):
            level_copy(piece, i).start()
        lax.fori_loop(0, 4, beams, 0)
        for i in range(1, BLOCKS):
            other = (place + i) % BLOCKS
            pltpu.make_async_remote_copy(
                level_send.at[piece], level_recv.at[piece, other], level_send_sem.at[piece, i - 1],
                level_recv_sem.at[piece, other],
                device_id={"section": other}, device_id_type=MESH,
            ).wait_recv()
        dividend = jnp.zeros((8, 128), f32)
        divisor = jnp.zeros((8, 128), f32)
        for block in range(BLOCKS):
            use = block <= place
            dividend = jnp.where(use, decay * dividend + level_recv[piece, block], dividend)
            divisor = jnp.where(use, decay * divisor + 1.0, divisor)
        scale = divisor / dividend

        def modulate(i, carry):
            for tile in range(2):
                lanes = slice(tile * 128, (tile + 1) * 128)
                frames = []
                for n in range(TDFT // 2):
                    later = power[i, n + TDFT // 2, :, lanes]
                    frames.append(power[i, n, :, lanes] - sign * later)
                freqs = []
                for q_even, q_odd in zip(evens, odds):
                    column_even = np.zeros(TDFT) if q_even is None else factors[:, q_even]
                    column_odd = factors[:, q_odd]
                    value = None
                    for n in range(TDFT // 2):
                        first, second = float(column_even[n]), float(column_odd[n])
                        if max(abs(first), abs(second)) < 1e-12:
                            continue
                        term = frames[n] * pair(first, second)
                        value = term if value is None else value + term
                    freqs.append(value * scale - pair(column_even.sum(), column_odd.sum()))
                for j, part in enumerate(exchange(freqs)):
                    send_two[piece, i * 16 + tile * 8 + j] = part.astype(bf16)
            return carry

        lax.fori_loop(0, 4, modulate, 0, unroll=piece == PIECES - 1)

        def two_plane(i, carry):
            z = plane_of(i)

            def one(r, inner):
                send_two_one(piece, z * 8 + (low + r) % 8)
                return inner

            return lax.fori_loop(0, 8, one, carry, unroll=piece == PIECES - 1)

        lax.fori_loop(0, 7, two_plane, 0)

        def two_last(r, carry):
            send_two_one(piece, my_z * 8 + (low + r) % 8)
            return carry

        lax.fori_loop(1, 8, two_last, 0)
        own_two[piece].start()

    for piece in range(PIECES):
        pltpu.make_async_remote_copy(
            recv_two.at[piece, pl.ds(0, SHARDS - 1)], recv_two.at[piece, pl.ds(0, SHARDS - 1)],
            send_two_sem.at[piece], recv_two_sem.at[piece],
            device_id={"shard": me}, device_id_type=MESH,
        ).wait_recv()
        own_two[piece].wait()
        data = recv_two[piece].astype(f32).reshape(SHARDS // 2, 2, 8, 128)
        first, second = data[:, 0], data[:, 1]
        mask = lower[None]
        split = (
            jnp.where(mask, first, pltpu.roll(second, QUARTER, 1)),
            jnp.where(mask, pltpu.roll(first, QUARTER, 1), second),
        )
        for side in range(2):
            turned[side] = split[side].reshape(SHARDS * QUARTER, 128).T.astype(bf16)

        def dedisperse(g, carry):
            side, at = (g + 1) % 2, g // 2
            real = turned[side, pl.ds(pl.multiple_of(at * LOCAL, LOCAL), LOCAL), :]
            imag = turned[side, pl.ds(pl.multiple_of((at + 3 + side) * LOCAL, LOCAL), LOCAL), :]
            rows = slice(piece * 256, (piece + 1) * 256)
            total = dot(jnp.concatenate([real, imag], 0), phase[g, 0, rows, :])
            total = total + dot(jnp.concatenate([imag, -real], 0), phase[g, 1, rows, :])
            if piece > 0:
                total = total + total_ref[g]
            if piece < PIECES - 1:
                total_ref[g] = total
            else:
                out_ref[g] = (total * (1.0 / math.sqrt(CHANS))).astype(bf16)
            return carry

        lax.fori_loop(0, MODF, dedisperse, 0, unroll=piece == PIECES - 1)

    for piece in range(PIECES):
        pltpu.make_async_remote_copy(
            send.at[piece, pl.ds(0, SHARDS - 1)], recv.at[piece, pl.ds(0, SHARDS - 1)],
            send_sem.at[piece], recv_sem.at[piece, 0],
            device_id={"shard": me}, device_id_type=MESH,
        ).wait_send()
        pltpu.make_async_remote_copy(
            send_two.at[piece, pl.ds(0, SHARDS - 1)], recv_two.at[piece, pl.ds(0, SHARDS - 1)],
            send_two_sem.at[piece], recv_two_sem.at[piece],
            device_id={"shard": me}, device_id_type=MESH,
        ).wait_send()
        for i in range(1, BLOCKS):
            level_copy(piece, i).wait_send()


def shards(voltages, feed_gains, grid_index, decay_rates, delays):
    bf16, f32 = jnp.bfloat16, jnp.float32
    far = pl.BlockSpec(memory_space=pltpu.HBM)
    here = pl.BlockSpec(memory_space=pltpu.VMEM)
    dma = pltpu.SemaphoreType.DMA
    out = pl.pallas_call(
        body,
        out_shape=jax.ShapeDtypeStruct((MODF, 2 * LOCAL, TRIALS), bf16),
        in_specs=[far] * 8,
        out_specs=here,
        scratch_shapes=[
            pltpu.VMEM((POL, LOCAL, TDFT * NSAMP), bf16),
            pltpu.VMEM((2, PIECE, NSAMP // 4), bf16),
            pltpu.VMEM((2, PIECE, NSAMP // 2), bf16),
            pltpu.VMEM((2, LOCAL, FEEDS), bf16),
            pltpu.VMEM((4, CHANS, 128), jnp.int32),
            pltpu.VMEM((8, 128), jnp.int32),
            pltpu.VMEM((1, LOCAL), f32),
            pltpu.VMEM((GRID_Y, 2 * GRID_Y), bf16),
            pltpu.VMEM((2, ROWS, NSAMP // 4), bf16),
            pltpu.VMEM((ROWS, NSAMP // 2), bf16),
            pltpu.VMEM((PIECES, SHARDS, LOCAL, ROWS // 2), bf16),
            pltpu.VMEM((PIECES, SHARDS, LOCAL, ROWS // 2), bf16),
            pltpu.VMEM((PIECES, 2, 8, FEEDS), f32),
            pltpu.VMEM((POL * TDFT * 8, FEEDS), bf16),
            pltpu.VMEM((2, FEEDS, FEEDS), bf16),
            pltpu.VMEM((MODF, 2, CHANS, TRIALS), bf16),
            pltpu.VMEM((4, TDFT, 8, 256), f32),
            pltpu.VMEM((PIECES, SHARDS, 8, 128), bf16),
            pltpu.VMEM((PIECES, SHARDS, 8, 128), bf16),
            pltpu.VMEM((2, 128, SHARDS * QUARTER), bf16),
            pltpu.VMEM((MODF, 2 * LOCAL, TRIALS), f32),
            pltpu.VMEM((PIECES, 8, 128), f32),
            pltpu.VMEM((PIECES, BLOCKS, 8, 128), f32),
            dma((14,)), dma((2 * PIECES,)), dma((PIECES,)), dma((PIECES, 8)), dma((PIECES,)),
            dma((PIECES,)), dma((PIECES, BLOCKS - 1)), dma((PIECES, BLOCKS)),
        ],
        compiler_params=pltpu.CompilerParams(
            collective_id=0, has_side_effects=True, vmem_limit_bytes=VMEM_LIMIT
        ),
        name="telescope",
    )(
        voltages[0], spectral_constant(CLASSES[:2], NSAMP // 4),
        spectral_constant(CLASSES[2:], NSAMP // 2), feed_gains, delays,
        grid_index.reshape(8, 128), decay_rates.reshape(1, LOCAL), row_constant(),
    )
    return out.reshape(MODF, 2, LOCAL, TRIALS).transpose(0, 3, 1, 2)[None]


def solution(mesh):
    in_specs = (P("section", None, "shard", None), P(None, "shard", None), P(), P("shard"), P())
    out_specs = P("section", None, None, None, "shard")
    return jax.shard_map(shards, mesh=mesh, in_specs=in_specs, out_specs=out_specs, check_vma=False)
```

```python
import math

import jax
import jax.numpy as jnp
import numpy as np
from jax import lax
from jax.experimental import pallas as pl
from jax.experimental.pallas import tpu as pltpu
from jax.sharding import PartitionSpec as P

POL = 2
GRID_X = 4
GRID_Y = 256
NSAMP = 2048
TDFT = 16
TRIALS = 512
FEEDS = 1024
CHANS = 1024
MODF = 7
BLOCKS = 4
SHARDS = 64
LOCAL = 16
QUARTER = LOCAL // 4
PIECES = 4
CLASSES = (0, 2, 1, 3)
ROWS = POL * TDFT * LOCAL
PIECE = SHARDS * 2 * QUARTER
VMEM_LIMIT = 62 * 1024 * 1024
MESH = pl.DeviceIdType.MESH


def spectral_constant(classes, length):
    shape = (len(classes), SHARDS, 2, QUARTER)
    which, dest, part, chan = np.meshgrid(*[np.arange(n) for n in shape], indexing="ij")
    chans = (dest * LOCAL + 4 * chan + np.asarray(classes)[which])[..., None].astype(np.int64)
    cols = np.arange(length, dtype=np.int64)
    angles = np.float32(2.0 * math.pi / NSAMP) * (chans * cols % NSAMP).astype(np.float32)
    table = np.where(part[..., None] == 0, np.cos(angles), -np.sin(angles)).astype(np.float32)
    return jnp.asarray(table.reshape(len(classes), PIECE, length)).astype(jnp.bfloat16)


def row_constant():
    rows = np.arange(GRID_Y)[:, None]
    cols = np.arange(GRID_Y)[None, :]
    angles = np.float32(2.0 * math.pi / GRID_Y) * (rows * cols % GRID_Y).astype(np.float32)
    table = np.concatenate([np.cos(angles), np.sin(angles)], 1).astype(np.float32)
    return jnp.asarray(table).astype(jnp.bfloat16)


def frame_matrix():
    frames = np.arange(TDFT)[:, None]
    freqs = np.arange(1, MODF + 1)[None, :]
    angles = 2.0 * math.pi / TDFT * (frames * freqs % TDFT)
    return np.concatenate([np.cos(angles), -np.sin(angles)], 1) / math.sqrt(TDFT)


def cosine_of(step):
    fold = jnp.abs(8 - step)
    out = jnp.full(step.shape, -math.cos(0.0), jnp.float32)
    for entry in range(1, 9):
        out = jnp.where(fold == entry, np.float32(-math.cos(2.0 * math.pi * entry / TDFT)), out)
    return out


def exchange(parts):
    parts = list(parts)
    lane = lax.broadcasted_iota(jnp.int32, parts[0].shape, 1)
    for bit in (4, 2, 1):
        upper = (lane & (bit * LOCAL)) != 0
        for i in range(8):
            if i & bit:
                continue
            low, high = parts[i], parts[i + bit]
            parts[i] = jnp.where(upper, pltpu.roll(high, bit * LOCAL, 1), low)
            parts[i + bit] = jnp.where(upper, high, pltpu.roll(low, 128 - bit * LOCAL, 1))
    return parts


def dot(a, b):
    return jnp.dot(a, b, preferred_element_type=jnp.float32)


def column(row):
    shape = (128, 128)
    same = lax.broadcasted_iota(jnp.int32, shape, 0) == lax.broadcasted_iota(jnp.int32, shape, 1)
    return jnp.sum(jnp.where(same, jnp.broadcast_to(row, shape), 0.0), axis=1, keepdims=True)


def body(
    volts_hbm, even_hbm, odd_hbm, gain_hbm, delay_hbm, cell_hbm, decay_hbm, row_hbm, out_ref,
    volts, even, odd, gain_in, delay, cell_ref, decay_ref, row_ref, fold_even, fold_odd, send, recv, gain, cal, beam_tab, phase, power,
    send_two, recv_two, turned, total_ref, level_send, level_recv,
    load_sem, own_sem, send_sem, recv_sem, send_two_sem, recv_two_sem, level_send_sem, level_recv_sem,
):
    f32, bf16 = jnp.float32, jnp.bfloat16
    me = lax.axis_index("shard")
    place = lax.axis_index("section")
    my_z, low = me // 8, me % 8

    load_volts = [
        pltpu.make_async_copy(volts_hbm.at[pol], volts.at[pol], load_sem.at[pol]) for pol in range(POL)
    ]
    load_even = [
        pltpu.make_async_copy(even_hbm.at[c], even.at[c], load_sem.at[2 + c]) for c in range(2)
    ]
    load_odd = [
        pltpu.make_async_copy(odd_hbm.at[c], odd.at[c], load_sem.at[4 + c]) for c in range(2)
    ]
    load_gain = pltpu.make_async_copy(gain_hbm, gain_in, load_sem.at[6])
    load_delay = [
        pltpu.make_async_copy(
            delay_hbm.at[:, pl.ds(tile * 128, 128)], delay.at[tile], load_sem.at[7 + tile]
        )
        for tile in range(4)
    ]
    load_small = [
        pltpu.make_async_copy(cell_hbm, cell_ref, load_sem.at[11]),
        pltpu.make_async_copy(decay_hbm, decay_ref, load_sem.at[12]),
        pltpu.make_async_copy(row_hbm, row_ref, load_sem.at[13]),
    ]
    for load in load_volts + load_even[:1]:
        load.start()

    barrier = pltpu.get_barrier_semaphore()

    def greet(i, carry):
        pl.semaphore_signal(barrier, inc=1, device_id={"shard": (me + i) % SHARDS}, device_id_type=MESH)
        return carry

    lax.fori_loop(1, SHARDS, greet, 0)
    for i in range(1, BLOCKS):
        pl.semaphore_signal(
            barrier, inc=1, device_id={"section": (place + i) % BLOCKS}, device_id_type=MESH
        )

    def quarters(pol, frame):
        parts = []
        for s in range(4):
            lanes = pl.ds(pl.multiple_of(frame * NSAMP + s * 512, 512), 512)
            parts.append(volts[pol, :, lanes].astype(f32))
        return parts, pl.ds(pl.multiple_of((pol * TDFT + frame) * LOCAL, LOCAL), LOCAL)

    def fold_sum(pol):
        def one(frame, carry):
            (a, b, c, d), rows = quarters(pol, frame)
            fold_even[0, rows, :] = ((a + c) + (b + d)).astype(bf16)
            fold_even[1, rows, :] = ((a + c) - (b + d)).astype(bf16)
            return carry

        lax.fori_loop(0, TDFT, one, 0)

    def fold_difference(pol):
        def one(frame, carry):
            (a, b, c, d), rows = quarters(pol, frame)
            fold_odd[rows, :512] = (a - c).astype(bf16)
            fold_odd[rows, 512:] = (b - d).astype(bf16)
            return carry

        lax.fori_loop(0, TDFT, one, 0)

    def plane_of(i):
        step, side = i // 2, i % 2
        return (my_z + 4 + step - side * (2 * step + 1) + 8) % 8

    def send_one(piece, dest):
        pltpu.make_async_remote_copy(
            send.at[piece, dest], recv.at[piece, me], send_sem.at[piece], recv_sem.at[piece, my_z],
            device_id={"shard": dest}, device_id_type=MESH,
        ).start()

    def send_plane(piece, i):
        z = plane_of(i)

        def one(r, carry):
            send_one(piece, z * 8 + (low + r) % 8)
            return carry

        lax.fori_loop(0, 8, one, 0)

    own = [
        pltpu.make_async_copy(send.at[piece, me], recv.at[piece, me], own_sem.at[piece])
        for piece in range(PIECES)
    ]

    def channelize(piece):
        def block(i, carry):
            z = (my_z // 2 + 2 + i) % 4
            rows = pl.ds(pl.multiple_of(z * 128, 128), 128)
            table, data = (even[piece, rows, :], fold_even[piece]) if piece < 2 else (
                odd[piece - 2, rows, :], fold_odd[...]
            )
            spectra = lax.dot_general(
                table, data, (((1,), (1,)), ((), ())), preferred_element_type=f32
            )
            spectra = (spectra * (1.0 / math.sqrt(NSAMP))).reshape(16, 8, ROWS)
            both = jnp.concatenate([spectra[:, :, : ROWS // 2], spectra[:, :, ROWS // 2 :]], 1)
            send[piece, pl.ds(pl.multiple_of(z * 16, 16), 16)] = both.astype(bf16)
            return carry

        lax.fori_loop(0, 4, block, 0)

    def send_piece(piece):
        def plane(i, carry):
            send_plane(piece, i)
            return carry

        lax.fori_loop(0, 7, plane, 0)

        def last(r, carry):
            send_one(piece, my_z * 8 + (low + r) % 8)
            return carry

        lax.fori_loop(1, 8, last, 0)
        own[piece].start()

    for pol in range(POL):
        load_volts[pol].wait()
        fold_sum(pol)
    load_even[0].wait()
    for load in load_even[1:] + load_odd + [load_gain] + load_small + load_delay:
        load.start()
    channelize(0)
    pl.semaphore_wait(barrier, SHARDS - 1 + BLOCKS - 1)
    send_piece(0)
    load_even[1].wait()
    channelize(1)
    send_piece(1)
    for pol in range(POL):
        fold_difference(pol)
    for piece in (2, 3):
        load_odd[piece - 2].wait()
        channelize(piece)
        send_piece(piece)

    def chan_pick(piece):
        shape = (8, LOCAL)
        row = lax.broadcasted_iota(jnp.int32, shape, 0) % QUARTER
        return lax.broadcasted_iota(jnp.int32, shape, 1) == 4 * row + CLASSES[piece]

    lower = lax.broadcasted_iota(jnp.int32, (8, 128), 0) < QUARTER
    sign = jnp.where(lower, -1.0, 1.0).astype(f32)

    load_gain.wait()
    for load in load_small:
        load.wait()
    for piece in range(PIECES):
        pick = chan_pick(piece).astype(f32).astype(bf16)
        gain[piece, 0] = dot(pick, gain_in[0])
        gain[piece, 1] = dot(pick, gain_in[1]) * sign[:, :1]

    def beam_rows(i, carry):
        cell = cell_ref[pl.ds(i, 1), :]
        x, y = cell // GRID_Y, cell % GRID_Y
        rows = pl.ds(pl.multiple_of(i * 128, 128), 128)
        y_column = column(y.astype(f32))
        lanes = lax.broadcasted_iota(jnp.int32, (128, GRID_Y), 1).astype(f32)
        hot = (lanes == y_column).astype(f32).astype(bf16)
        both = dot(hot, row_ref[...])
        cos, sin = both[:, :GRID_Y], both[:, GRID_Y:]
        for u in range(GRID_X):
            turn = column(((u * x) % 4).astype(f32))
            real = jnp.where(turn == 0, cos, jnp.where(turn == 1, -sin, jnp.where(turn == 2, -cos, sin)))
            imag = jnp.where(turn == 0, -sin, jnp.where(turn == 1, -cos, jnp.where(turn == 2, sin, cos)))
            beam_tab[0, rows, u * GRID_Y : (u + 1) * GRID_Y] = real.astype(bf16)
            beam_tab[1, rows, u * GRID_Y : (u + 1) * GRID_Y] = imag.astype(bf16)
        return carry

    lax.fori_loop(0, 8, beam_rows, 0)

    for load in load_delay:
        load.wait()
    for piece in range(PIECES):

        def phases(i, carry):
            tile, block = i // 4, i % 4
            step = delay[tile, pl.ds(CLASSES[piece] + 256 * block, 64, stride=4), :] & (TDFT - 1)
            rows = pl.ds(pl.multiple_of(piece * 256 + block * 64, 64), 64)
            lanes = pl.ds(pl.multiple_of(tile * 128, 128), 128)
            parity = (1 - 2 * (step & 1)).astype(f32)
            cos, sin = cosine_of(step), cosine_of((step + 12) & (TDFT - 1))
            twice = 2.0 * cos
            cos_now, sin_now = cos, sin
            cos_last, sin_last = jnp.ones_like(cos), jnp.zeros_like(cos)
            for f in range(1, 5):
                phase[f - 1, 0, rows, lanes] = cos_now.astype(bf16)
                phase[f - 1, 1, rows, lanes] = sin_now.astype(bf16)
                if f < 4:
                    phase[7 - f, 0, rows, lanes] = (parity * cos_now).astype(bf16)
                    phase[7 - f, 1, rows, lanes] = (-parity * sin_now).astype(bf16)
                    cos_now, cos_last = twice * cos_now - cos_last, cos_now
                    sin_now, sin_last = twice * sin_now - sin_last, sin_now
            return carry

        lax.fori_loop(0, 16, phases, 0)

    def calibrate(piece, octet):
        feeds = pl.ds(pl.multiple_of(octet * 128, 128), 128)
        straight, crossed = gain[piece, 0, :, feeds], gain[piece, 1, :, feeds]

        def one(tile, total):
            lanes = pl.ds(pl.multiple_of(tile * 128, 128), 128)
            parts = [recv[piece, octet * 8 + s, :, lanes].astype(f32) for s in range(8)]
            parts = exchange(parts)
            for pol in range(POL):
                values = []
                for part in parts:
                    value = part[pol * 8 : pol * 8 + 8]
                    values.append(straight * value + crossed * pltpu.roll(value, QUARTER, 0))
                for n in range(0, 8, 2):
                    rows = pl.ds(pl.multiple_of(pol * 128 + tile * 64 + n * 8, LOCAL), LOCAL)
                    value = jnp.concatenate(values[n : n + 2], 0).astype(bf16)
                    cal[rows, feeds] = value
                    wide = value.astype(f32)
                    total = total + wide * wide
            return total

        return lax.fori_loop(0, 2, one, jnp.zeros((LOCAL, 128), f32), unroll=True)

    def arrive(piece, octet, count):
        pltpu.make_async_remote_copy(
            recv.at[piece, pl.ds(0, count)], recv.at[piece, pl.ds(0, count)],
            send_sem.at[piece], recv_sem.at[piece, octet],
            device_id={"shard": me}, device_id_type=MESH,
        ).wait_recv()

    def level_copy(piece, i):
        return pltpu.make_async_remote_copy(
            level_send.at[piece], level_recv.at[piece, place], level_send_sem.at[piece, i - 1],
            level_recv_sem.at[piece, place],
            device_id={"section": (place + i) % BLOCKS}, device_id_type=MESH,
        )

    def send_two_one(piece, dest):
        pltpu.make_async_remote_copy(
            send_two.at[piece, dest], recv_two.at[piece, me], send_two_sem.at[piece],
            recv_two_sem.at[piece], device_id={"shard": dest}, device_id_type=MESH,
        ).start()

    own_two = [
        pltpu.make_async_copy(
            send_two.at[piece, me], recv_two.at[piece, me], own_sem.at[PIECES + piece]
        )
        for piece in range(PIECES)
    ]
    factors = frame_matrix()
    evens = [1, 3, 5, 1 + MODF, 3 + MODF, 5 + MODF, None, None]
    odds = [0, 2, 4, 6, MODF, 2 + MODF, 4 + MODF, 6 + MODF]

    def pair(first, second):
        return jnp.where(lower, np.float32(first), np.float32(second))

    for piece in range(PIECES):

        def octets(i, total):
            octet = plane_of(i)
            arrive(piece, octet, 8)
            return total + calibrate(piece, octet)

        total = lax.fori_loop(0, 7, octets, jnp.zeros((LOCAL, 128), f32))
        arrive(piece, my_z, 7)
        own[piece].wait()
        total = total + calibrate(piece, my_z)
        total = total[:8] + total[8:]
        total = total + pltpu.roll(total, QUARTER, 0)
        total = jnp.sum(total, axis=1, keepdims=True) * (1.0 / TDFT) + 1e-06
        level_send[piece] = jnp.broadcast_to(total, (8, 128))
        level_recv[piece, place] = jnp.broadcast_to(total, (8, 128))

        decay_row = jnp.broadcast_to(decay_ref[...], (8, LOCAL))
        decay = jnp.sum(jnp.where(chan_pick(piece), decay_row, 0.0), axis=1, keepdims=True)
        decay = jnp.broadcast_to(decay, (8, 128))

        def beams(i, carry):
            wide = pl.ds(pl.multiple_of(i * 256, 256), 256)
            straight = dot(cal[...], beam_tab[0, :, wide]).reshape(32, 8, 256)
            crossed = dot(cal[...], beam_tab[1, :, wide]).reshape(32, 8, 256)
            value = straight + pltpu.roll(crossed, QUARTER, 1) * sign[:, :1]
            value = value * value
            value = value[:TDFT] + value[TDFT:]
            power[i] = value + pltpu.roll(value, QUARTER, 1)
            return carry

        for i in range(1, BLOCKS):
            level_copy(piece, i).start()
        lax.fori_loop(0, 4, beams, 0)
        for i in range(1, BLOCKS):
            other = (place + i) % BLOCKS
            pltpu.make_async_remote_copy(
                level_send.at[piece], level_recv.at[piece, other], level_send_sem.at[piece, i - 1],
                level_recv_sem.at[piece, other],
                device_id={"section": other}, device_id_type=MESH,
            ).wait_recv()
        dividend = jnp.zeros((8, 128), f32)
        divisor = jnp.zeros((8, 128), f32)
        for block in range(BLOCKS):
            use = block <= place
            dividend = jnp.where(use, decay * dividend + level_recv[piece, block], dividend)
            divisor = jnp.where(use, decay * divisor + 1.0, divisor)
        scale = divisor / dividend

        def modulate(i, carry):
            for tile in range(2):
                lanes = slice(tile * 128, (tile + 1) * 128)
                frames = []
                for n in range(TDFT // 2):
                    later = power[i, n + TDFT // 2, :, lanes]
                    frames.append(power[i, n, :, lanes] - sign * later)
                freqs = []
                for q_even, q_odd in zip(evens, odds):
                    column_even = np.zeros(TDFT) if q_even is None else factors[:, q_even]
                    column_odd = factors[:, q_odd]
                    value = None
                    for n in range(TDFT // 2):
                        first, second = float(column_even[n]), float(column_odd[n])
                        if max(abs(first), abs(second)) < 1e-12:
                            continue
                        term = frames[n] * pair(first, second)
                        value = term if value is None else value + term
                    freqs.append(value * scale - pair(column_even.sum(), column_odd.sum()))
                for j, part in enumerate(exchange(freqs)):
                    send_two[piece, i * 16 + tile * 8 + j] = part.astype(bf16)
            return carry

        lax.fori_loop(0, 4, modulate, 0, unroll=piece == PIECES - 1)

        def two_plane(i, carry):
            z = plane_of(i)

            def one(r, inner):
                send_two_one(piece, z * 8 + (low + r) % 8)
                return inner

            return lax.fori_loop(0, 8, one, carry, unroll=piece == PIECES - 1)

        lax.fori_loop(0, 7, two_plane, 0)

        def two_last(r, carry):
            send_two_one(piece, my_z * 8 + (low + r) % 8)
            return carry

        lax.fori_loop(1, 8, two_last, 0)
        own_two[piece].start()

    for piece in range(PIECES):
        pltpu.make_async_remote_copy(
            recv_two.at[piece, pl.ds(0, SHARDS - 1)], recv_two.at[piece, pl.ds(0, SHARDS - 1)],
            send_two_sem.at[piece], recv_two_sem.at[piece],
            device_id={"shard": me}, device_id_type=MESH,
        ).wait_recv()
        own_two[piece].wait()
        data = recv_two[piece].astype(f32).reshape(SHARDS // 2, 2, 8, 128)
        first, second = data[:, 0], data[:, 1]
        mask = lower[None]
        split = (
            jnp.where(mask, first, pltpu.roll(second, QUARTER, 1)),
            jnp.where(mask, pltpu.roll(first, QUARTER, 1), second),
        )
        for side in range(2):
            turned[side] = split[side].reshape(SHARDS * QUARTER, 128).T.astype(bf16)

        def dedisperse(g, carry):
            side, at = (g + 1) % 2, g // 2
            real = turned[side, pl.ds(pl.multiple_of(at * LOCAL, LOCAL), LOCAL), :]
            imag = turned[side, pl.ds(pl.multiple_of((at + 3 + side) * LOCAL, LOCAL), LOCAL), :]
            rows = slice(piece * 256, (piece + 1) * 256)
            total = dot(jnp.concatenate([real, imag], 0), phase[g, 0, rows, :])
            total = total + dot(jnp.concatenate([imag, -real], 0), phase[g, 1, rows, :])
            if piece > 0:
                total = total + total_ref[g]
            if piece < PIECES - 1:
                total_ref[g] = total
            else:
                out_ref[g] = (total * (1.0 / math.sqrt(CHANS))).astype(bf16)
            return carry

        lax.fori_loop(0, MODF, dedisperse, 0, unroll=piece == PIECES - 1)

    for piece in range(PIECES):
        pltpu.make_async_remote_copy(
            send.at[piece, pl.ds(0, SHARDS - 1)], recv.at[piece, pl.ds(0, SHARDS - 1)],
            send_sem.at[piece], recv_sem.at[piece, 0],
            device_id={"shard": me}, device_id_type=MESH,
        ).wait_send()
        pltpu.make_async_remote_copy(
            send_two.at[piece, pl.ds(0, SHARDS - 1)], recv_two.at[piece, pl.ds(0, SHARDS - 1)],
            send_two_sem.at[piece], recv_two_sem.at[piece],
            device_id={"shard": me}, device_id_type=MESH,
        ).wait_send()
        for i in range(1, BLOCKS):
            level_copy(piece, i).wait_send()


def shards(voltages, feed_gains, grid_index, decay_rates, delays):
    bf16, f32 = jnp.bfloat16, jnp.float32
    far = pl.BlockSpec(memory_space=pltpu.HBM)
    here = pl.BlockSpec(memory_space=pltpu.VMEM)
    dma = pltpu.SemaphoreType.DMA
    out = pl.pallas_call(
        body,
        out_shape=jax.ShapeDtypeStruct((MODF, 2 * LOCAL, TRIALS), bf16),
        in_specs=[far] * 8,
        out_specs=here,
        scratch_shapes=[
            pltpu.VMEM((POL, LOCAL, TDFT * NSAMP), bf16),
            pltpu.VMEM((2, PIECE, NSAMP // 4), bf16),
            pltpu.VMEM((2, PIECE, NSAMP // 2), bf16),
            pltpu.VMEM((2, LOCAL, FEEDS), bf16),
            pltpu.VMEM((4, CHANS, 128), jnp.int32),
            pltpu.VMEM((8, 128), jnp.int32),
            pltpu.VMEM((1, LOCAL), f32),
            pltpu.VMEM((GRID_Y, 2 * GRID_Y), bf16),
            pltpu.VMEM((2, ROWS, NSAMP // 4), bf16),
            pltpu.VMEM((ROWS, NSAMP // 2), bf16),
            pltpu.VMEM((PIECES, SHARDS, LOCAL, ROWS // 2), bf16),
            pltpu.VMEM((PIECES, SHARDS, LOCAL, ROWS // 2), bf16),
            pltpu.VMEM((PIECES, 2, 8, FEEDS), f32),
            pltpu.VMEM((POL * TDFT * 8, FEEDS), bf16),
            pltpu.VMEM((2, FEEDS, FEEDS), bf16),
            pltpu.VMEM((MODF, 2, CHANS, TRIALS), bf16),
            pltpu.VMEM((4, TDFT, 8, 256), f32),
            pltpu.VMEM((PIECES, SHARDS, 8, 128), bf16),
            pltpu.VMEM((PIECES, SHARDS, 8, 128), bf16),
            pltpu.VMEM((2, 128, SHARDS * QUARTER), bf16),
            pltpu.VMEM((MODF, 2 * LOCAL, TRIALS), f32),
            pltpu.VMEM((PIECES, 8, 128), f32),
            pltpu.VMEM((PIECES, BLOCKS, 8, 128), f32),
            dma((14,)), dma((2 * PIECES,)), dma((PIECES,)), dma((PIECES, 8)), dma((PIECES,)),
            dma((PIECES,)), dma((PIECES, BLOCKS - 1)), dma((PIECES, BLOCKS)),
        ],
        compiler_params=pltpu.CompilerParams(
            collective_id=0, has_side_effects=True, vmem_limit_bytes=VMEM_LIMIT
        ),
        name="telescope",
    )(
        voltages[0], spectral_constant(CLASSES[:2], NSAMP // 4),
        spectral_constant(CLASSES[2:], NSAMP // 2), feed_gains, delays,
        grid_index.reshape(8, 128), decay_rates.reshape(1, LOCAL), row_constant(),
    )
    return out.reshape(MODF, 2, LOCAL, TRIALS).transpose(0, 3, 1, 2)[None]


def solution(mesh):
    in_specs = (P("section", None, "shard", None), P(None, "shard", None), P(), P("shard"), P())
    out_specs = P("section", None, None, None, "shard")
    return jax.shard_map(shards, mesh=mesh, in_specs=in_specs, out_specs=out_specs, check_vma=False)
```

```python
import math

import jax
import jax.numpy as jnp
import numpy as np
from jax import lax
from jax.experimental import pallas as pl
from jax.experimental.pallas import tpu as pltpu
from jax.sharding import PartitionSpec as P

POL = 2
GRID_X = 4
GRID_Y = 256
NSAMP = 2048
TDFT = 16
TRIALS = 512
FEEDS = 1024
CHANS = 1024
MODF = 7
BLOCKS = 4
SHARDS = 64
LOCAL = 16
QUARTER = LOCAL // 4
PIECES = 4
CLASSES = (0, 2, 1, 3)
ROWS = POL * TDFT * LOCAL
PIECE = SHARDS * 2 * QUARTER
VMEM_LIMIT = 62 * 1024 * 1024
MESH = pl.DeviceIdType.MESH


def spectral_constant(classes, length):
    shape = (len(classes), SHARDS, 2, QUARTER)
    which, dest, part, chan = np.meshgrid(*[np.arange(n) for n in shape], indexing="ij")
    chans = (dest * LOCAL + 4 * chan + np.asarray(classes)[which])[..., None].astype(np.int64)
    cols = np.arange(length, dtype=np.int64)
    angles = np.float32(2.0 * math.pi / NSAMP) * (chans * cols % NSAMP).astype(np.float32)
    table = np.where(part[..., None] == 0, np.cos(angles), -np.sin(angles)).astype(np.float32)
    return jnp.asarray(table.reshape(len(classes), PIECE, length)).astype(jnp.bfloat16)


def row_constant():
    rows = np.arange(GRID_Y)[:, None]
    cols = np.arange(GRID_Y)[None, :]
    angles = np.float32(2.0 * math.pi / GRID_Y) * (rows * cols % GRID_Y).astype(np.float32)
    table = np.concatenate([np.cos(angles), np.sin(angles)], 1).astype(np.float32)
    return jnp.asarray(table).astype(jnp.bfloat16)


def frame_matrix():
    frames = np.arange(TDFT)[:, None]
    freqs = np.arange(1, MODF + 1)[None, :]
    angles = 2.0 * math.pi / TDFT * (frames * freqs % TDFT)
    return np.concatenate([np.cos(angles), -np.sin(angles)], 1) / math.sqrt(TDFT)


def cosine_of(step):
    fold = jnp.abs(8 - step)
    out = jnp.full(step.shape, -math.cos(0.0), jnp.float32)
    for entry in range(1, 9):
        out = jnp.where(fold == entry, np.float32(-math.cos(2.0 * math.pi * entry / TDFT)), out)
    return out


def exchange(parts):
    parts = list(parts)
    lane = lax.broadcasted_iota(jnp.int32, parts[0].shape, 1)
    for bit in (4, 2, 1):
        upper = (lane & (bit * LOCAL)) != 0
        for i in range(8):
            if i & bit:
                continue
            low, high = parts[i], parts[i + bit]
            parts[i] = jnp.where(upper, pltpu.roll(high, bit * LOCAL, 1), low)
            parts[i + bit] = jnp.where(upper, high, pltpu.roll(low, 128 - bit * LOCAL, 1))
    return parts


def dot(a, b):
    return jnp.dot(a, b, preferred_element_type=jnp.float32)


def column(row):
    shape = (128, 128)
    same = lax.broadcasted_iota(jnp.int32, shape, 0) == lax.broadcasted_iota(jnp.int32, shape, 1)
    return jnp.sum(jnp.where(same, jnp.broadcast_to(row, shape), 0.0), axis=1, keepdims=True)


def body(
    volts_hbm, even_hbm, odd_hbm, gain_hbm, delay_hbm, cell_hbm, decay_hbm, row_hbm, out_ref,
    volts, even, odd, gain_in, delay, cell_ref, decay_ref, row_ref, fold_even, fold_odd, send, recv, gain, cal, beam_tab, phase, power,
    send_two, recv_two, turned, total_ref, level_send, level_recv,
    load_sem, own_sem, send_sem, recv_sem, send_two_sem, recv_two_sem, level_send_sem, level_recv_sem,
):
    f32, bf16 = jnp.float32, jnp.bfloat16
    me = lax.axis_index("shard")
    place = lax.axis_index("section")
    my_z, low = me // 8, me % 8

    load_volts = [
        pltpu.make_async_copy(volts_hbm.at[pol], volts.at[pol], load_sem.at[pol]) for pol in range(POL)
    ]
    load_even = [
        pltpu.make_async_copy(even_hbm.at[c], even.at[c], load_sem.at[2 + c]) for c in range(2)
    ]
    load_odd = [
        pltpu.make_async_copy(odd_hbm.at[c], odd.at[c], load_sem.at[4 + c]) for c in range(2)
    ]
    load_gain = pltpu.make_async_copy(gain_hbm, gain_in, load_sem.at[6])
    load_delay = [
        pltpu.make_async_copy(
            delay_hbm.at[:, pl.ds(tile * 128, 128)], delay.at[tile, pl.ds(0, CHANS)],
            load_sem.at[7 + tile],
        )
        for tile in range(4)
    ]
    load_small = [
        pltpu.make_async_copy(cell_hbm, cell_ref.at[pl.ds(0, 8)], load_sem.at[11]),
        pltpu.make_async_copy(decay_hbm, decay_ref, load_sem.at[12]),
        pltpu.make_async_copy(row_hbm, row_ref, load_sem.at[13]),
    ]
    for load in load_volts + load_even[:1]:
        load.start()

    barrier = pltpu.get_barrier_semaphore()

    def greet(i, carry):
        pl.semaphore_signal(barrier, inc=1, device_id={"shard": (me + i) % SHARDS}, device_id_type=MESH)
        return carry

    lax.fori_loop(1, SHARDS, greet, 0)
    for i in range(1, BLOCKS):
        pl.semaphore_signal(
            barrier, inc=1, device_id={"section": (place + i) % BLOCKS}, device_id_type=MESH
        )

    def quarters(pol, frame):
        parts = []
        for s in range(4):
            lanes = pl.ds(pl.multiple_of(frame * NSAMP + s * 512, 512), 512)
            parts.append(volts[pol, :, lanes].astype(f32))
        return parts, pl.ds(pl.multiple_of((pol * TDFT + frame) * LOCAL, LOCAL), LOCAL)

    def fold_sum(pol):
        def one(frame, carry):
            (a, b, c, d), rows = quarters(pol, frame)
            fold_even[0, rows, :] = ((a + c) + (b + d)).astype(bf16)
            fold_even[1, rows, :] = ((a + c) - (b + d)).astype(bf16)
            return carry

        lax.fori_loop(0, TDFT, one, 0)

    def fold_difference(pol):
        def one(frame, carry):
            (a, b, c, d), rows = quarters(pol, frame)
            fold_odd[rows, :512] = (a - c).astype(bf16)
            fold_odd[rows, 512:] = (b - d).astype(bf16)
            return carry

        lax.fori_loop(0, TDFT, one, 0)

    def plane_of(i):
        step, side = i // 2, i % 2
        return (my_z + 4 + step - side * (2 * step + 1) + 8) % 8

    def send_one(piece, dest):
        pltpu.make_async_remote_copy(
            send.at[piece, dest], recv.at[piece, me], send_sem.at[piece], recv_sem.at[piece, my_z],
            device_id={"shard": dest}, device_id_type=MESH,
        ).start()

    def send_plane(piece, i):
        z = plane_of(i)

        def one(r, carry):
            send_one(piece, z * 8 + (low + r) % 8)
            return carry

        lax.fori_loop(0, 8, one, 0)

    own = [
        pltpu.make_async_copy(send.at[piece, me], recv.at[piece, me], own_sem.at[piece])
        for piece in range(PIECES)
    ]

    def channelize(piece):
        def block(i, carry):
            z = (my_z // 2 + 2 + i) % 4
            rows = pl.ds(pl.multiple_of(z * 128, 128), 128)
            table, data = (even[piece, rows, :], fold_even[piece]) if piece < 2 else (
                odd[piece - 2, rows, :], fold_odd[...]
            )
            spectra = lax.dot_general(
                table, data, (((1,), (1,)), ((), ())), preferred_element_type=f32
            )
            spectra = (spectra * (1.0 / math.sqrt(NSAMP))).reshape(16, 8, ROWS)
            both = jnp.concatenate([spectra[:, :, : ROWS // 2], spectra[:, :, ROWS // 2 :]], 1)
            send[piece, pl.ds(pl.multiple_of(z * 16, 16), 16)] = both.astype(bf16)
            return carry

        lax.fori_loop(0, 4, block, 0)

    def send_piece(piece):
        def plane(i, carry):
            send_plane(piece, i)
            return carry

        lax.fori_loop(0, 7, plane, 0)

        def last(r, carry):
            send_one(piece, my_z * 8 + (low + r) % 8)
            return carry

        lax.fori_loop(1, 8, last, 0)
        own[piece].start()

    for pol in range(POL):
        load_volts[pol].wait()
        fold_sum(pol)
    load_even[0].wait()
    for load in load_even[1:] + load_odd + [load_gain] + load_small + load_delay:
        load.start()
    channelize(0)
    pl.semaphore_wait(barrier, SHARDS - 1 + BLOCKS - 1)
    send_piece(0)
    load_even[1].wait()
    channelize(1)
    send_piece(1)
    for pol in range(POL):
        fold_difference(pol)
    for piece in (2, 3):
        load_odd[piece - 2].wait()
        channelize(piece)
        send_piece(piece)

    def chan_pick(piece):
        shape = (8, LOCAL)
        row = lax.broadcasted_iota(jnp.int32, shape, 0) % QUARTER
        return lax.broadcasted_iota(jnp.int32, shape, 1) == 4 * row + CLASSES[piece]

    lower = lax.broadcasted_iota(jnp.int32, (8, 128), 0) < QUARTER
    sign = jnp.where(lower, -1.0, 1.0).astype(f32)

    load_gain.wait()
    for load in load_small:
        load.wait()
    for piece in range(PIECES):
        pick = chan_pick(piece).astype(f32).astype(bf16)
        gain[piece, 0] = dot(pick, gain_in[0])
        gain[piece, 1] = dot(pick, gain_in[1]) * sign[:, :1]

    def beam_rows(i, carry):
        cell = cell_ref[pl.ds(i, 1), :]
        x, y = cell // GRID_Y, cell % GRID_Y
        rows = pl.ds(pl.multiple_of(i * 128, 128), 128)
        y_column = column(y.astype(f32))
        lanes = lax.broadcasted_iota(jnp.int32, (128, GRID_Y), 1).astype(f32)
        hot = (lanes == y_column).astype(f32).astype(bf16)
        both = dot(hot, row_ref[...])
        cos, sin = both[:, :GRID_Y], both[:, GRID_Y:]
        for u in range(GRID_X):
            turn = column(((u * x) % 4).astype(f32))
            real = jnp.where(turn == 0, cos, jnp.where(turn == 1, -sin, jnp.where(turn == 2, -cos, sin)))
            imag = jnp.where(turn == 0, -sin, jnp.where(turn == 1, -cos, jnp.where(turn == 2, sin, cos)))
            beam_tab[0, rows, u * GRID_Y : (u + 1) * GRID_Y] = real.astype(bf16)
            beam_tab[1, rows, u * GRID_Y : (u + 1) * GRID_Y] = imag.astype(bf16)
        return carry

    lax.fori_loop(0, 8, beam_rows, 0)

    for load in load_delay:
        load.wait()
    for piece in range(PIECES):

        def phases(i, carry):
            tile, block = i // 4, i % 4
            step = delay[tile, pl.ds(CLASSES[piece] + 256 * block, 64, stride=4), :] & (TDFT - 1)
            rows = pl.ds(pl.multiple_of(piece * 256 + block * 64, 64), 64)
            lanes = pl.ds(pl.multiple_of(tile * 128, 128), 128)
            parity = (1 - 2 * (step & 1)).astype(f32)
            cos, sin = cosine_of(step), cosine_of((step + 12) & (TDFT - 1))
            twice = 2.0 * cos
            cos_now, sin_now = cos, sin
            cos_last, sin_last = jnp.ones_like(cos), jnp.zeros_like(cos)
            for f in range(1, 5):
                phase[f - 1, 0, rows, lanes] = cos_now.astype(bf16)
                phase[f - 1, 1, rows, lanes] = sin_now.astype(bf16)
                if f < 4:
                    phase[7 - f, 0, rows, lanes] = (parity * cos_now).astype(bf16)
                    phase[7 - f, 1, rows, lanes] = (-parity * sin_now).astype(bf16)
                    cos_now, cos_last = twice * cos_now - cos_last, cos_now
                    sin_now, sin_last = twice * sin_now - sin_last, sin_now
            return carry

        lax.fori_loop(0, 16, phases, 0)

    def calibrate(piece, octet):
        feeds = pl.ds(pl.multiple_of(octet * 128, 128), 128)
        straight, crossed = gain[piece, 0, :, feeds], gain[piece, 1, :, feeds]

        def one(tile, total):
            lanes = pl.ds(pl.multiple_of(tile * 128, 128), 128)
            parts = [recv[piece, octet * 8 + s, :, lanes].astype(f32) for s in range(8)]
            parts = exchange(parts)
            for pol in range(POL):
                values = []
                for part in parts:
                    value = part[pol * 8 : pol * 8 + 8]
                    values.append(straight * value + crossed * pltpu.roll(value, QUARTER, 0))
                for n in range(0, 8, 2):
                    rows = pl.ds(pl.multiple_of(pol * 128 + tile * 64 + n * 8, LOCAL), LOCAL)
                    value = jnp.concatenate(values[n : n + 2], 0).astype(bf16)
                    cal[rows, feeds] = value
                    wide = value.astype(f32)
                    total = total + wide * wide
            return total

        return lax.fori_loop(0, 2, one, jnp.zeros((LOCAL, 128), f32), unroll=True)

    def arrive(piece, octet, count):
        pltpu.make_async_remote_copy(
            recv.at[piece, pl.ds(0, count)], recv.at[piece, pl.ds(0, count)],
            send_sem.at[piece], recv_sem.at[piece, octet],
            device_id={"shard": me}, device_id_type=MESH,
        ).wait_recv()

    def level_copy(piece, i):
        return pltpu.make_async_remote_copy(
            level_send.at[piece], level_recv.at[piece, place], level_send_sem.at[piece, i - 1],
            level_recv_sem.at[piece, place],
            device_id={"section": (place + i) % BLOCKS}, device_id_type=MESH,
        )

    def send_two_one(piece, dest):
        pltpu.make_async_remote_copy(
            send_two.at[piece, dest], recv_two.at[piece, me], send_two_sem.at[piece],
            recv_two_sem.at[piece], device_id={"shard": dest}, device_id_type=MESH,
        ).start()

    own_two = [
        pltpu.make_async_copy(
            send_two.at[piece, me], recv_two.at[piece, me], own_sem.at[PIECES + piece]
        )
        for piece in range(PIECES)
    ]
    factors = frame_matrix()
    evens = [1, 3, 5, 1 + MODF, 3 + MODF, 5 + MODF, None, None]
    odds = [0, 2, 4, 6, MODF, 2 + MODF, 4 + MODF, 6 + MODF]

    def pair(first, second):
        return jnp.where(lower, np.float32(first), np.float32(second))

    for piece in range(PIECES):

        def octets(i, total):
            octet = plane_of(i)
            arrive(piece, octet, 8)
            return total + calibrate(piece, octet)

        total = lax.fori_loop(0, 7, octets, jnp.zeros((LOCAL, 128), f32))
        arrive(piece, my_z, 7)
        own[piece].wait()
        total = total + calibrate(piece, my_z)
        total = total[:8] + total[8:]
        total = total + pltpu.roll(total, QUARTER, 0)
        total = jnp.sum(total, axis=1, keepdims=True) * (1.0 / TDFT) + 1e-06
        level_send[piece] = jnp.broadcast_to(total, (8, 128))
        level_recv[piece, place] = jnp.broadcast_to(total, (8, 128))

        decay_row = jnp.broadcast_to(decay_ref[...], (8, LOCAL))
        decay = jnp.sum(jnp.where(chan_pick(piece), decay_row, 0.0), axis=1, keepdims=True)
        decay = jnp.broadcast_to(decay, (8, 128))

        def beams(i, carry):
            wide = pl.ds(pl.multiple_of(i * 256, 256), 256)
            straight = dot(cal[...], beam_tab[0, :, wide]).reshape(32, 8, 256)
            crossed = dot(cal[...], beam_tab[1, :, wide]).reshape(32, 8, 256)
            value = straight + pltpu.roll(crossed, QUARTER, 1) * sign[:, :1]
            value = value * value
            value = value[:TDFT] + value[TDFT:]
            power[i] = value + pltpu.roll(value, QUARTER, 1)
            return carry

        for i in range(1, BLOCKS):
            level_copy(piece, i).start()
        lax.fori_loop(0, 4, beams, 0)
        for i in range(1, BLOCKS):
            other = (place + i) % BLOCKS
            pltpu.make_async_remote_copy(
                level_send.at[piece], level_recv.at[piece, other], level_send_sem.at[piece, i - 1],
                level_recv_sem.at[piece, other],
                device_id={"section": other}, device_id_type=MESH,
            ).wait_recv()
        dividend = jnp.zeros((8, 128), f32)
        divisor = jnp.zeros((8, 128), f32)
        for block in range(BLOCKS):
            use = block <= place
            dividend = jnp.where(use, decay * dividend + level_recv[piece, block], dividend)
            divisor = jnp.where(use, decay * divisor + 1.0, divisor)
        scale = divisor / dividend

        def modulate(i, carry):
            for tile in range(2):
                lanes = slice(tile * 128, (tile + 1) * 128)
                frames = []
                for n in range(TDFT // 2):
                    later = power[i, n + TDFT // 2, :, lanes]
                    frames.append(power[i, n, :, lanes] - sign * later)
                freqs = []
                for q_even, q_odd in zip(evens, odds):
                    column_even = np.zeros(TDFT) if q_even is None else factors[:, q_even]
                    column_odd = factors[:, q_odd]
                    value = None
                    for n in range(TDFT // 2):
                        first, second = float(column_even[n]), float(column_odd[n])
                        if max(abs(first), abs(second)) < 1e-12:
                            continue
                        term = frames[n] * pair(first, second)
                        value = term if value is None else value + term
                    freqs.append(value * scale - pair(column_even.sum(), column_odd.sum()))
                for j, part in enumerate(exchange(freqs)):
                    send_two[piece, i * 16 + tile * 8 + j] = part.astype(bf16)
            return carry

        lax.fori_loop(0, 4, modulate, 0, unroll=piece == PIECES - 1)

        def two_plane(i, carry):
            z = plane_of(i)

            def one(r, inner):
                send_two_one(piece, z * 8 + (low + r) % 8)
                return inner

            return lax.fori_loop(0, 8, one, carry, unroll=piece == PIECES - 1)

        lax.fori_loop(0, 7, two_plane, 0)

        def two_last(r, carry):
            send_two_one(piece, my_z * 8 + (low + r) % 8)
            return carry

        lax.fori_loop(1, 8, two_last, 0)
        own_two[piece].start()

    for piece in range(PIECES):
        pltpu.make_async_remote_copy(
            recv_two.at[piece, pl.ds(0, SHARDS - 1)], recv_two.at[piece, pl.ds(0, SHARDS - 1)],
            send_two_sem.at[piece], recv_two_sem.at[piece],
            device_id={"shard": me}, device_id_type=MESH,
        ).wait_recv()
        own_two[piece].wait()
        data = recv_two[piece].astype(f32).reshape(SHARDS // 2, 2, 8, 128)
        first, second = data[:, 0], data[:, 1]
        mask = lower[None]
        split = (
            jnp.where(mask, first, pltpu.roll(second, QUARTER, 1)),
            jnp.where(mask, pltpu.roll(first, QUARTER, 1), second),
        )
        for side in range(2):
            turned[side] = split[side].reshape(SHARDS * QUARTER, 128).T.astype(bf16)

        def dedisperse(g, carry):
            side, at = (g + 1) % 2, g // 2
            real = turned[side, pl.ds(pl.multiple_of(at * LOCAL, LOCAL), LOCAL), :]
            imag = turned[side, pl.ds(pl.multiple_of((at + 3 + side) * LOCAL, LOCAL), LOCAL), :]
            rows = slice(piece * 256, (piece + 1) * 256)
            total = dot(jnp.concatenate([real, imag], 0), phase[g, 0, rows, :])
            total = total + dot(jnp.concatenate([imag, -real], 0), phase[g, 1, rows, :])
            if piece > 0:
                total = total + total_ref[g]
            if piece < PIECES - 1:
                total_ref[g] = total
            else:
                out_ref[g] = (total * (1.0 / math.sqrt(CHANS))).astype(bf16)
            return carry

        lax.fori_loop(0, MODF, dedisperse, 0, unroll=piece >= PIECES - 2)

    for piece in range(PIECES):
        pltpu.make_async_remote_copy(
            send.at[piece, pl.ds(0, SHARDS - 1)], recv.at[piece, pl.ds(0, SHARDS - 1)],
            send_sem.at[piece], recv_sem.at[piece, 0],
            device_id={"shard": me}, device_id_type=MESH,
        ).wait_send()
        pltpu.make_async_remote_copy(
            send_two.at[piece, pl.ds(0, SHARDS - 1)], recv_two.at[piece, pl.ds(0, SHARDS - 1)],
            send_two_sem.at[piece], recv_two_sem.at[piece],
            device_id={"shard": me}, device_id_type=MESH,
        ).wait_send()
        for i in range(1, BLOCKS):
            level_copy(piece, i).wait_send()


def shards(voltages, feed_gains, grid_index, decay_rates, delays):
    bf16, f32 = jnp.bfloat16, jnp.float32
    far = pl.BlockSpec(memory_space=pltpu.HBM)
    here = pl.BlockSpec(memory_space=pltpu.VMEM)
    dma = pltpu.SemaphoreType.DMA
    out = pl.pallas_call(
        body,
        out_shape=jax.ShapeDtypeStruct((MODF, 2 * LOCAL, TRIALS), bf16),
        in_specs=[far] * 8,
        out_specs=here,
        scratch_shapes=[
            pltpu.VMEM((POL, LOCAL, TDFT * NSAMP), bf16),
            pltpu.VMEM((2, PIECE, NSAMP // 4), bf16),
            pltpu.VMEM((2, PIECE, NSAMP // 2), bf16),
            pltpu.VMEM((2, LOCAL, FEEDS), bf16),
            pltpu.VMEM((4, CHANS + 8, 128), jnp.int32),
            pltpu.VMEM((16, 128), jnp.int32),
            pltpu.VMEM((1, LOCAL), f32),
            pltpu.VMEM((GRID_Y, 2 * GRID_Y), bf16),
            pltpu.VMEM((2, ROWS, NSAMP // 4), bf16),
            pltpu.VMEM((ROWS, NSAMP // 2), bf16),
            pltpu.VMEM((PIECES, SHARDS, LOCAL, ROWS // 2), bf16),
            pltpu.VMEM((PIECES, SHARDS, LOCAL, ROWS // 2), bf16),
            pltpu.VMEM((PIECES, 2, 8, FEEDS), f32),
            pltpu.VMEM((POL * TDFT * 8, FEEDS), bf16),
            pltpu.VMEM((2, FEEDS, FEEDS), bf16),
            pltpu.VMEM((MODF, 2, CHANS, TRIALS), bf16),
            pltpu.VMEM((4, TDFT, 8, 256), f32),
            pltpu.VMEM((PIECES, SHARDS, 8, 128), bf16),
            pltpu.VMEM((PIECES, SHARDS, 8, 128), bf16),
            pltpu.VMEM((2, 128, SHARDS * QUARTER), bf16),
            pltpu.VMEM((MODF, 2 * LOCAL, TRIALS), f32),
            pltpu.VMEM((PIECES, 8, 128), f32),
            pltpu.VMEM((PIECES, BLOCKS, 8, 128), f32),
            dma((14,)), dma((2 * PIECES,)), dma((PIECES,)), dma((PIECES, 8)), dma((PIECES,)),
            dma((PIECES,)), dma((PIECES, BLOCKS - 1)), dma((PIECES, BLOCKS)),
        ],
        compiler_params=pltpu.CompilerParams(
            collective_id=0, has_side_effects=True, vmem_limit_bytes=VMEM_LIMIT
        ),
        name="telescope",
    )(
        voltages[0], spectral_constant(CLASSES[:2], NSAMP // 4),
        spectral_constant(CLASSES[2:], NSAMP // 2), feed_gains, delays,
        grid_index.reshape(8, 128), decay_rates.reshape(1, LOCAL), row_constant(),
    )
    return out.reshape(MODF, 2, LOCAL, TRIALS).transpose(0, 3, 1, 2)[None]


def solution(mesh):
    in_specs = (P("section", None, "shard", None), P(None, "shard", None), P(), P("shard"), P())
    out_specs = P("section", None, None, None, "shard")
    return jax.shard_map(shards, mesh=mesh, in_specs=in_specs, out_specs=out_specs, check_vma=False)
```
